512 devices in a mesh: tm: 16 (over x, z_hi, core), coef: 32 (over y, z_lo).
Axes of the slice: x: 4, y: 8, z: 8 (z_hi: 2, z_lo: 4; z = z_hi * 4 + z_lo), core: 2. Of those that a mesh axis runs over, the one named last changes fastest.
Arguments:
- design: float32 [8192, 40960], P('tm', 'coef'), may hold values from -4 to 4
- whitening: float32 [8192, 256], P('tm'), may hold values from -1 to 3, as said below
- solution: float32 [40960, 64], P('coef'), may hold values from -6 to 6
- direction: float32 [40960, 64], P('coef'), may hold values from -6 to 6
- gradient_prev: float32 [40960, 64], P('coef'), may hold values from -25 to 25
- residual: float32 [8192, 64], P('tm'), may hold values from -6 to 6
Outputs:
- new_solution: float32 [40960, 64], P('coef')
- new_residual: float32 [8192, 64], P('tm')
- new_direction: float32 [40960, 64], P('coef')
The draws below stay inside these ranges and needn't reach their ends.
Inputs may be any that keep to these rules, and one draw needn't show every extreme that they name: `whitening`: the first tap of every row is positive.
All inputs are finite; a program needn't handle non-finite values.
Results may differ from the reference program's by a relative error of at most 0.00008.
Values sent between devices are 32-bit elements; how exact they have to be, the bound alone decides.
No kernel may reach another device: no remote copies, remote signals or barrier semaphores. Data moves between devices by JAX's collectives and lax.ppermute only.
A program may use at most 64 MiB of HBM per device.

```python
import math
import jax
import jax.numpy as jnp
from jax import lax

NC = 40960
R = 64
BW = 256
ROWS = 8192


def column_scales(key_scale, count):
    rising = 3.0 ** (jnp.arange(count, dtype=jnp.float32) / count)
    return jnp.exp(jax.random.uniform(key_scale, (count,), jnp.float32) * math.log(10.0)) * rising


def draw_whitening(key, part):
    key_scale = jax.random.fold_in(key, 11)
    key_lead = jax.random.fold_in(key, 12)
    key_tail = jax.random.fold_in(key, 13)
    row_scale = column_scales(key_scale, ROWS)[:, None] * 0.033
    leading = jax.random.uniform(key_lead, (ROWS, 1), jnp.float32, 1.0, 2.0)
    trailing = jnp.clip(jax.random.normal(key_tail, (ROWS, BW - 1), jnp.float32), -4.0, 4.0) * 0.05
    return jnp.concatenate([leading, trailing], axis=1) * row_scale


def draw_design(key, part):
    key_scale = jax.random.fold_in(key, 21)
    key_base = jax.random.fold_in(key, 22)
    scales = column_scales(key_scale, NC)[None, :] / (2.2 * math.sqrt(NC))
    base_values = jnp.clip(jax.random.normal(key_base, (ROWS, NC), jnp.float32), -4.0, 4.0)
    return base_values * scales


def draw_gradient_prev(key, part):
    key_scale = jax.random.fold_in(key, 31)
    key_base = jax.random.fold_in(key, 32)
    scales = column_scales(key_scale, NC)[:, None] * 0.145
    base_values = jnp.clip(jax.random.normal(key_base, (NC, R), jnp.float32), -4.0, 4.0)
    return base_values * scales


def block_levels(rng, extent, pieces, low, largest):
    def one(axis_at, blocks):
        heights = jax.random.uniform(jax.random.fold_in(jax.random.fold_in(rng, 6), axis_at), (blocks,), jnp.float32, low / len(pieces), largest / len(pieces))
        return jnp.repeat(jnp.exp(heights), extent[axis_at] // blocks).reshape((-1,) + (1,) * (len(extent) - axis_at - 1))

    gain = one(*pieces[0])
    for cut in pieces[1:]:
        gain = gain * one(*cut)
    return gain


def gaussian(own_key, shape, deviation, most, shards=(), kind=jnp.bfloat16):
    entries = deviation * jax.random.normal(own_key, shape, jnp.float32)
    if shards:
        entries = entries * block_levels(own_key, shape, shards, -0.22, 0.18)
    return jnp.clip(entries, -most, most).astype(kind)


def setup_inputs(seed: int = 0) -> dict:
    seeds = jax.random.split(jax.random.key(seed), 7)
    return {
        "design": draw_design(jax.random.fold_in(seeds[6], 71), 0),
        "whitening": draw_whitening(jax.random.fold_in(seeds[6], 71), 0),
        "solution": gaussian(seeds[2], (NC, R), 1.0, 6.0, ((0, 32),), jnp.float32),
        "direction": gaussian(seeds[3], (NC, R), 1.0, 6.0, ((0, 32),), jnp.float32),
        "gradient_prev": draw_gradient_prev(jax.random.fold_in(seeds[6], 71), 0),
        "residual": gaussian(seeds[5], (ROWS, R), 1.0, 6.0, ((0, 16),), jnp.float32),
    }


def whiten(values, taps):
    rows_all = values.shape[0]
    lag = taps.shape[1]
    padded = jnp.concatenate([jnp.zeros((lag - 1, values.shape[1]), values.dtype), values], axis=0)

    def add_tap(offset, total):
        start = (lag - 1 - offset).astype(jnp.int32)
        shifted = lax.dynamic_slice_in_dim(padded, start, rows_all, 0)
        column = lax.dynamic_slice_in_dim(taps, offset.astype(jnp.int32), 1, 1)
        return total + column * shifted

    return lax.fori_loop(jnp.int32(0), jnp.int32(lag), add_tap, jnp.zeros_like(values))


def unwhiten(values, taps):
    rows_all = values.shape[0]
    lag = taps.shape[1]
    tail_zeros = jnp.zeros((lag - 1, values.shape[1]), values.dtype)

    def add_tap(offset, total):
        column = lax.dynamic_slice_in_dim(taps, offset.astype(jnp.int32), 1, 1)
        padded = jnp.concatenate([column * values, tail_zeros], axis=0)
        return total + lax.dynamic_slice_in_dim(padded, offset.astype(jnp.int32), rows_all, 0)

    return lax.fori_loop(jnp.int32(0), jnp.int32(lag), add_tap, jnp.zeros_like(values))


def reference(design, whitening, solution, direction, gradient_prev, residual):
    old_norm = jnp.sum(gradient_prev * gradient_prev, axis=0)
    plain = jnp.dot(design, direction, precision=lax.Precision.HIGHEST, preferred_element_type=jnp.float32)
    predicted = whiten(plain, whitening)
    energy = jnp.sum(predicted * predicted, axis=0)
    step_size = old_norm / energy
    new_solution = solution + step_size * direction
    new_residual = residual - step_size * predicted
    whitened = unwhiten(new_residual, whitening)
    gradient = lax.dot_general(design, whitened, (((0,), (0,)), ((), ())), precision=lax.Precision.HIGHEST, preferred_element_type=jnp.float32)
    new_norm = jnp.sum(gradient * gradient, axis=0)
    new_direction = gradient + (new_norm / old_norm) * direction
    return new_solution, new_residual, new_direction
```

```python
import jax
import jax.numpy as jnp
from jax import lax
from jax.experimental import pallas as pl
from jax.experimental.pallas import tpu as pltpu
from jax.sharding import PartitionSpec as P

HIGHEST = lax.Precision.HIGHEST
BLOCK = 256


def dot_nn(a, b):
    return lax.dot_general(a, b, (((1,), (0,)), ((), ())), precision=HIGHEST, preferred_element_type=jnp.float32)


def dot_nt(a, b):
    return lax.dot_general(a, b, (((1,), (1,)), ((), ())), precision=HIGHEST, preferred_element_type=jnp.float32)


def skew(rows):
    return pltpu.roll(rows, 0, 1, stride=1, stride_axis=0)


def row_sums(values):
    padded = jnp.concatenate([values, jnp.zeros_like(values)], axis=0)
    return dot_nt(jnp.ones((8, values.shape[1]), jnp.float32), padded)


def as_column(row, first, count):
    shape = (count, 128)
    pick = lax.broadcasted_iota(jnp.int32, shape, 1) == lax.broadcasted_iota(jnp.int32, shape, 0) + first
    return jnp.sum(jnp.where(pick, jnp.broadcast_to(row[:1], shape), 0.0), axis=1, keepdims=True)


def predict_part(direction, design, gradient_prev):
    part = dot_nt(direction, design)
    tiles = [part[8 * j : 8 * j + 8, 128 * i : 128 * i + 128] for j in range(8) for i in range(4)]
    return jnp.stack(tiles), row_sums(gradient_prev * gradient_prev)


def band(whitening, rim, residual):
    taps = jnp.concatenate([whitening, rim[:BLOCK]], axis=0)
    lag = lax.broadcasted_iota(jnp.int32, (BLOCK, BLOCK), 0)
    lane = lax.broadcasted_iota(jnp.int32, (BLOCK, BLOCK), 1)
    mirror = jnp.where((lag + lane) % BLOCK == 0, 1.0, 0.0)
    mirrored = dot_nn(taps, mirror)
    same, before = [], []
    for b in range(3):
        full = skew(mirrored[BLOCK * b : BLOCK * (b + 1)])
        same.append(jnp.where(lane <= lag, full, 0.0))
        before.append(jnp.where(lane > lag, full, 0.0))
    res = [residual[:, :BLOCK], residual[:, BLOCK:], rim[BLOCK:]]
    back = [dot_nn(res[b], same[b]) + dot_nn(res[b + 1], before[b + 1]) for b in range(2)]
    return jnp.stack(same), jnp.stack(before), jnp.concatenate(back, axis=1)


def whiten_and_project(gathered, same, before, back, design):
    def block(halves, rows):
        return jnp.concatenate(
            [jnp.concatenate([gathered[4 * j + i][rows : rows + 8] for i in halves], axis=1) for j in range(8)], axis=0
        )

    plain = [block((2, 3), 8), block((0, 1), 0), block((2, 3), 0), block((0, 1), 8)]
    old = gathered[0][16:24]
    for m in range(1, 32):
        old = old + gathered[m][16:24]
    pred = [dot_nt(plain[b + 1], same[b]) + dot_nt(plain[b], before[b]) for b in range(3)]
    own = jnp.concatenate(pred[:2], axis=1)
    energy = row_sums(own * own)
    spread = [dot_nn(pred[b], same[b]) + dot_nn(pred[b + 1], before[b + 1]) for b in range(2)]
    both = jnp.concatenate([back, jnp.concatenate(spread, axis=1)], axis=0)
    grad = dot_nn(both, design)
    count = grad.shape[1] // 2
    pieces = []
    for j in range(8):
        for h in range(2):
            cut = slice(count * h, count * (h + 1))
            pieces.append(jnp.concatenate([grad[8 * j : 8 * j + 8, cut], grad[64 + 8 * j : 72 + 8 * j, cut], energy], axis=1))
    return jnp.stack(pieces), own, old


def step_piece(place, parts, old):
    total = parts[0]
    for m in range(1, parts.shape[0]):
        total = total + parts[m]
    count = (total.shape[1] - 128) // 2
    alpha = old / total[:, 2 * count :]
    alpha = jnp.where(lax.broadcasted_iota(jnp.int32, alpha.shape, 1) < 64, alpha, 0.0)
    grad = total[:, :count] - as_column(alpha, 8 * (place[0] // 2), 8) * total[:, count : 2 * count]
    return jnp.broadcast_to(grad[None], parts.shape[:1] + grad.shape), alpha


def assemble(pieces):
    return jnp.concatenate([jnp.concatenate([pieces[2 * j], pieces[2 * j + 1]], axis=1) for j in range(8)], axis=0)


def norm_part(pieces):
    grad = assemble(pieces)
    norm = row_sums(grad * grad)
    return jnp.broadcast_to(norm[None, :1], (32, 1, 128))


def finish(norms, pieces, old, alpha, solution, direction, residual, predicted):
    norm = norms[0]
    for m in range(1, norms.shape[0]):
        norm = norm + norms[m]
    step = as_column(alpha, 0, 64)
    beta = as_column(norm, 0, 64) / as_column(old, 0, 64)
    return (
        solution + step * direction,
        residual - step * predicted,
        assemble(pieces) + beta * direction,
    )


def run(function, outs, *args, scalar=False):
    def kernel(*refs):
        values = [refs[0] if scalar and k == 0 else r[...] for k, r in enumerate(refs[: len(args)])]
        results = function(*values)
        results = results if isinstance(results, tuple) else (results,)
        for ref, value in zip(refs[len(args) :], results, strict=True):
            ref[...] = value

    spaces = [pltpu.SMEM if scalar and k == 0 else pltpu.VMEM for k in range(len(args))]
    got = pl.pallas_call(
        kernel,
        out_shape=[jax.ShapeDtypeStruct(s, jnp.float32) for s in outs],
        in_specs=[pl.BlockSpec(memory_space=s) for s in spaces],
        out_specs=[pl.BlockSpec(memory_space=pltpu.VMEM) for _ in outs],
        name=function.__name__,
    )(*args)
    return got if len(outs) > 1 else got[0]


def exchange(array, axis):
    return lax.all_to_all(array, axis, 0, 0, tiled=True)


def per_device(design, whitening, solution, direction, gradient_prev, residual):
    blocks_t, blocks_c = lax.axis_size("tm"), lax.axis_size("coef")
    coefs = design.shape[1]
    solution, direction, gradient_prev, residual = solution.T, direction.T, gradient_prev.T, residual.T
    rim = lax.ppermute(
        jnp.concatenate([whitening[:BLOCK], residual[:, :BLOCK]], axis=0),
        "tm",
        [(i + 1, i) for i in range(blocks_t - 1)],
    )
    parts, old_part = run(predict_part, [(32, 8, 128), (8, 128)], direction, design, gradient_prev)
    tile = jnp.sum(exchange(parts, "coef"), axis=0)
    pairs = []
    for t in range(blocks_t):
        for c in range(blocks_c):
            to = t + 1 if c % 4 >= 2 else t - 1
            if 0 <= to < blocks_t:
                pairs.append((t * blocks_c + c, to * blocks_c + c))
    rim_tile = lax.ppermute(tile, ("tm", "coef"), pairs)
    same, before, back = run(
        band, [(3, BLOCK, BLOCK), (3, BLOCK, BLOCK), residual.shape], whitening, rim, residual
    )
    chunk = jnp.concatenate([tile, rim_tile, old_part], axis=0)
    gathered = exchange(jnp.broadcast_to(chunk[None], (blocks_c,) + chunk.shape), "coef")
    pieces, predicted, old = run(
        whiten_and_project,
        [(16, 8, coefs + 128), residual.shape, (8, 128)],
        gathered,
        same,
        before,
        back,
        design,
    )
    place = lax.axis_index("tm").astype(jnp.int32)[None]
    grad_piece, alpha = run(
        step_piece, [(16, 8, coefs // 2), (8, 128)], place, exchange(pieces, "tm"), old, scalar=True
    )
    pieces = exchange(grad_piece, "tm")
    norms = exchange(run(norm_part, [(32, 1, 128)], pieces), "coef")
    outs = run(
        finish,
        [solution.shape, residual.shape, direction.shape],
        norms,
        pieces,
        old,
        alpha,
        solution,
        direction,
        residual,
        predicted,
    )
    return tuple(out.T for out in outs)


def solution(mesh):
    return jax.shard_map(
        per_device,
        mesh=mesh,
        in_specs=(
            P("tm", "coef"),
            P("tm", None),
            P("coef", None),
            P("coef", None),
            P("coef", None),
            P("tm", None),
        ),
        out_specs=(P("coef", None), P("tm", None), P("coef", None)),
        check_vma=False,
    )
```

```python
import jax
import jax.numpy as jnp
from jax import lax
from jax.experimental import pallas as pl
from jax.experimental.pallas import tpu as pltpu
from jax.sharding import PartitionSpec as P


HIGHEST = lax.Precision.HIGHEST
BLOCK = 256


def dot_nn(a, b):
    return lax.dot_general(a, b, (((1,), (0,)), ((), ())), precision=HIGHEST, preferred_element_type=jnp.float32)


def dot_nt(a, b):
    return lax.dot_general(a, b, (((1,), (1,)), ((), ())), precision=HIGHEST, preferred_element_type=jnp.float32)


def skew(rows):
    return pltpu.roll(rows, 0, 1, stride=1, stride_axis=0)


def row_sums(values):
    padded = jnp.concatenate([values, jnp.zeros_like(values)], axis=0)
    return dot_nt(jnp.ones((8, values.shape[1]), jnp.float32), padded)


def as_column(row, first, count):
    shape = (count, 128)
    pick = lax.broadcasted_iota(jnp.int32, shape, 1) == lax.broadcasted_iota(jnp.int32, shape, 0) + first
    return jnp.sum(jnp.where(pick, jnp.broadcast_to(row[:1], shape), 0.0), axis=1, keepdims=True)


def predict_part(direction, design, gradient_prev):
    part = dot_nt(direction, design)
    old = row_sums(gradient_prev * gradient_prev)[:1]
    rows = []
    for j in range(8):
        for i in range(4):
            rows += [part[8 * j : 8 * j + 8, 128 * i : 128 * i + 128], old]
    return jnp.concatenate(rows, axis=0)


def collect(rows):
    tile, old = rows[:8], rows[8:9]
    for m in range(1, 32):
        tile = tile + rows[9 * m : 9 * m + 8]
        old = old + rows[9 * m + 8 : 9 * m + 9]
    return tile, jnp.broadcast_to(old, (8, 128))


def chunk(tile, rim):
    return jnp.concatenate([tile, rim] * 32, axis=0)


def band(whitening, rim, residual, design):
    taps = jnp.concatenate([whitening, rim[:BLOCK]], axis=0)
    lag = lax.broadcasted_iota(jnp.int32, (BLOCK, BLOCK), 0)
    lane = lax.broadcasted_iota(jnp.int32, (BLOCK, BLOCK), 1)
    mirror = jnp.where((lag + lane) % BLOCK == 0, 1.0, 0.0)
    mirrored = dot_nn(taps, mirror)
    same, before = [], []
    for b in range(3):
        full = skew(mirrored[BLOCK * b : BLOCK * (b + 1)])
        same.append(jnp.where(lane <= lag, full, 0.0))
        before.append(jnp.where(lane > lag, full, 0.0))
    res = [residual[:, :BLOCK], residual[:, BLOCK:], rim[BLOCK:]]
    back = [dot_nn(res[b], same[b]) + dot_nn(res[b + 1], before[b + 1]) for b in range(2)]
    return jnp.stack(same), jnp.stack(before), dot_nn(jnp.concatenate(back, axis=1), design)


def whiten_and_project(gathered, same, before, back_grad, design):
    def block(halves, row):
        return jnp.concatenate(
            [
                jnp.concatenate([gathered[16 * m + row : 16 * m + row + 8] for m in (4 * j + i for i in halves)], axis=1)
                for j in range(8)
            ],
            axis=0,
        )

    plain = [block((2, 3), 8), block((0, 1), 0), block((2, 3), 0), block((0, 1), 8)]
    pred = [dot_nt(plain[b + 1], same[b]) + dot_nt(plain[b], before[b]) for b in range(3)]
    own = jnp.concatenate(pred[:2], axis=1)
    energy = row_sums(own * own)
    spread = [dot_nn(pred[b], same[b]) + dot_nn(pred[b + 1], before[b + 1]) for b in range(2)]
    grad = dot_nn(jnp.concatenate(spread, axis=1), design)
    return jnp.concatenate([back_grad, grad, jnp.concatenate([energy] * 8, axis=0)], axis=1), own


def sum_pieces(pieces):
    total = pieces[:8]
    for m in range(1, 8):
        total = total + pieces[8 * m : 8 * m + 8]
    return total


def step_piece(place, mine, other, old):
    total = mine + other
    count = (total.shape[1] - 128) // 2
    alpha = old / total[:, 2 * count :]
    alpha = jnp.where(lax.broadcasted_iota(jnp.int32, alpha.shape, 1) < 64, alpha, 0.0)
    grad = total[:, :count] - as_column(alpha, 8 * place[0], 8) * total[:, count : 2 * count]
    norm = jnp.sum(grad * grad, axis=1, keepdims=True)
    shape = (8, 128)
    pick = lax.broadcasted_iota(jnp.int32, shape, 0) == lax.broadcasted_iota(jnp.int32, shape, 1)
    row = jnp.sum(jnp.where(pick, jnp.broadcast_to(norm, shape), 0.0), axis=0, keepdims=True)
    return grad, alpha, jnp.broadcast_to(row, (32, 128))


def direction_piece(place, norms, grad, old, direction):
    norm = jnp.sum(norms, axis=0, keepdims=True)
    beta = as_column(norm, 0, 8) / as_column(old, 8 * place[0], 8)
    mine = direction[pl.ds(pl.multiple_of(8 * place[0], 8), 8), :]
    return jnp.concatenate([grad + beta * mine] * 8, axis=0)


def update(alpha, solution, direction, residual, predicted):
    step = as_column(alpha, 0, 64)
    return solution + step * direction, residual - step * predicted


def run(function, outs, *args, scalar=False, keep=()):
    def kernel(*refs):
        values = [r if k in keep else r[...] for k, r in enumerate(refs[: len(args)])]
        results = function(*values)
        results = results if isinstance(results, tuple) else (results,)
        for ref, value in zip(refs[len(args) :], results, strict=True):
            ref[...] = value

    spaces = [pltpu.SMEM if scalar and k == 0 else pltpu.VMEM for k in range(len(args))]
    got = pl.pallas_call(
        kernel,
        out_shape=[jax.ShapeDtypeStruct(s, jnp.float32) for s in outs],
        in_specs=[pl.BlockSpec(memory_space=s) for s in spaces],
        out_specs=[pl.BlockSpec(memory_space=pltpu.VMEM) for _ in outs],
    )(*args)
    return got if len(outs) > 1 else got[0]


def exchange(rows, axis, groups=None):
    return lax.all_to_all(rows, axis, 0, 0, axis_index_groups=groups, tiled=True)


def per_device(design, whitening, solution, direction, gradient_prev, residual):
    blocks_t, blocks_c = lax.axis_size("tm"), lax.axis_size("coef")
    coefs = design.shape[1]
    solution, direction, gradient_prev, residual = solution.T, direction.T, gradient_prev.T, residual.T
    groups = [[4 * x + 2 * z + k for x in range(4) for k in range(2)] for z in range(2)]
    t = lax.axis_index("tm").astype(jnp.int32)
    place = (lax.shift_right_logical(t, 2) * 2 + (t & 1))[None]
    rim = lax.ppermute(
        jnp.concatenate([whitening[:BLOCK], residual[:, :BLOCK]], axis=0),
        "tm",
        [(i + 1, i) for i in range(blocks_t - 1)],
    )
    rows = run(predict_part, [(9 * 32, 128)], direction, design, gradient_prev)
    rows = exchange(rows.reshape(32, 9 * 128), "coef").reshape(9 * 32, 128)
    same, before, back_grad = run(
        band,
        [(3, BLOCK, BLOCK), (3, BLOCK, BLOCK), (64, coefs)],
        whitening,
        rim,
        residual,
        design,
    )
    rows, same, before, back_grad = lax.optimization_barrier((rows, same, before, back_grad))
    tile, old = run(collect, [(8, 128), (8, 128)], rows)
    pairs = []
    for t in range(blocks_t):
        for c in range(blocks_c):
            to = t + 1 if c % 4 >= 2 else t - 1
            if 0 <= to < blocks_t:
                pairs.append((t * blocks_c + c, to * blocks_c + c))
    rim_tile = lax.ppermute(tile, ("tm", "coef"), pairs)
    gathered = exchange(run(chunk, [(16 * 32, 128)], tile, rim_tile), "coef")
    pieces, predicted = run(
        whiten_and_project,
        [(64, 2 * coefs + 128), residual.shape],
        gathered,
        same,
        before,
        back_grad,
        design,
    )
    mine = run(sum_pieces, [(8, 2 * coefs + 128)], exchange(pieces, "tm", groups))
    other = lax.ppermute(mine, "tm", [(i, i ^ 2) for i in range(blocks_t)])
    grad, alpha, norms = run(
        step_piece, [(8, coefs), (8, 128), (32, 128)], place, mine, other, old, scalar=True, keep=(0,)
    )
    norms = exchange(norms, "coef")
    new_solution, new_residual = run(
        update, [solution.shape, residual.shape], alpha, solution, direction, residual, predicted
    )
    pieces = run(
        direction_piece, [(64, coefs)], place, norms, grad, old, direction, scalar=True, keep=(0, 4)
    )
    return new_solution.T, new_residual.T, exchange(pieces, "tm", groups).T


def solution(mesh):
    return jax.shard_map(
        per_device,
        mesh=mesh,
        in_specs=(
            P("tm", "coef"),
            P("tm", None),
            P("coef", None),
            P("coef", None),
            P("coef", None),
            P("tm", None),
        ),
        out_specs=(P("coef", None), P("tm", None), P("coef", None)),
        check_vma=False,
    )
```

```python
import jax
import jax.numpy as jnp
from jax import lax
from jax.experimental import pallas as pl
from jax.experimental.pallas import tpu as pltpu
from jax.sharding import PartitionSpec as P


BLOCK = 256
NN = (((1,), (0,)), ((), ()))
NT = (((1,), (1,)), ((), ()))
F32, BF16 = jnp.float32, jnp.bfloat16


def split(values):
    high = values.astype(BF16)
    return high, (values - high.astype(F32)).astype(BF16)


def times(left, right, dims):
    high, low = split(left)
    count = left.shape[0]
    first = lax.dot_general(jnp.concatenate([high, low], axis=0), right[0], dims, preferred_element_type=F32)
    return first[:count] + first[count:] + lax.dot_general(high, right[1], dims, preferred_element_type=F32)


def skew(rows):
    return pltpu.roll(rows, 0, 1, stride=1, stride_axis=0)


def as_row(column):
    shape = (column.shape[0], 128)
    pick = lax.broadcasted_iota(jnp.int32, shape, 0) == lax.broadcasted_iota(jnp.int32, shape, 1)
    return jnp.sum(jnp.where(pick, jnp.broadcast_to(column, shape), 0.0), axis=0, keepdims=True)


def row_squares(values):
    total = values[:, :128] * values[:, :128]
    for k in range(128, values.shape[1], 128):
        total = total + values[:, k : k + 128] * values[:, k : k + 128]
    return as_row(jnp.sum(total, axis=1, keepdims=True))


def as_column(row, first, count):
    shape = (count, 128)
    pick = lax.broadcasted_iota(jnp.int32, shape, 1) == lax.broadcasted_iota(jnp.int32, shape, 0) + first
    return jnp.sum(jnp.where(pick, jnp.broadcast_to(row[:1], shape), 0.0), axis=1, keepdims=True)


def collect(rows):
    tile, old = rows[:8], rows[8:9]
    for m in range(1, 32):
        tile = tile + rows[9 * m : 9 * m + 8]
        old = old + rows[9 * m + 8 : 9 * m + 9]
    return tile, jnp.broadcast_to(old, (8, 128))


def chunk(tile, rim):
    return jnp.concatenate([tile, rim] * 32, axis=0)


def band(whitening, rim, residual, design):
    taps = jnp.concatenate([whitening, rim[:BLOCK]], axis=0)
    lag = lax.broadcasted_iota(jnp.int32, (BLOCK, BLOCK), 0)
    lane = lax.broadcasted_iota(jnp.int32, (BLOCK, BLOCK), 1)
    mirror = jnp.where((lag + lane) % BLOCK == 0, 1.0, 0.0).astype(BF16)
    high, low = split(taps)
    least = (taps - high.astype(F32) - low.astype(F32)).astype(BF16)
    count = taps.shape[0]
    turned = lax.dot_general(jnp.concatenate([high, low, least], axis=0), mirror, NN, preferred_element_type=F32)
    turned = turned[:count] + turned[count : 2 * count] + turned[2 * count :]
    same, before = [], []
    for b in range(3):
        full = skew(turned[BLOCK * b : BLOCK * (b + 1)])
        same.append(split(jnp.where(lane <= lag, full, 0.0)))
        before.append(split(jnp.where(lane > lag, full, 0.0)))
    res = [residual[:, :BLOCK], residual[:, BLOCK:], rim[BLOCK:]]
    back = [times(res[b], same[b], NN) + times(res[b + 1], before[b + 1], NN) for b in range(2)]
    bands = [jnp.stack([m[k] for m in kind]) for kind in (same, before) for k in range(2)]
    return *bands, times(jnp.concatenate(back, axis=1), split(design()), NN)


def whiten_and_project(gathered, same_high, same_low, before_high, before_low, back_grad, design):
    def block(halves, row):
        return jnp.concatenate(
            [
                jnp.concatenate([gathered[16 * m + row : 16 * m + row + 8] for m in (4 * j + i for i in halves)], axis=1)
                for j in range(8)
            ],
            axis=0,
        )

    same = [(same_high[b], same_low[b]) for b in range(3)]
    before = [(before_high[b], before_low[b]) for b in range(3)]
    plain = [block((2, 3), 8), block((0, 1), 0), block((2, 3), 0), block((0, 1), 8)]
    pred = [times(plain[b + 1], same[b], NT) + times(plain[b], before[b], NT) for b in range(3)]
    own = jnp.concatenate(pred[:2], axis=1)
    energy = jnp.broadcast_to(row_squares(own), (64, 128))
    spread = [times(pred[b], same[b], NN) + times(pred[b + 1], before[b + 1], NN) for b in range(2)]
    grad = times(jnp.concatenate(spread, axis=1), split(design()), NN)
    return jnp.concatenate([back_grad, grad, energy], axis=1), own


def sum_pieces(pieces):
    total = pieces[:8]
    for m in range(1, 8):
        total = total + pieces[8 * m : 8 * m + 8]
    return total


def step_piece(place, mine, other, old):
    total = mine + other
    count = (total.shape[1] - 128) // 2
    alpha = old / total[:, 2 * count :]
    alpha = jnp.where(lax.broadcasted_iota(jnp.int32, alpha.shape, 1) < 64, alpha, 0.0)
    grad = total[:, :count] - as_column(alpha, 8 * place[0], 8) * total[:, count : 2 * count]
    return grad, alpha, jnp.broadcast_to(row_squares(grad), (32, 128))


def direction_piece(place, norms, grad, old, direction):
    norm = jnp.sum(norms, axis=0, keepdims=True)
    beta = as_column(norm, 0, 8) / as_column(old, 8 * place[0], 8)
    mine = direction[pl.ds(pl.multiple_of(8 * place[0], 8), 8), :]
    return jnp.concatenate([grad + beta * mine] * 8, axis=0)


def update(alpha, solution, direction, residual, predicted):
    step = as_column(alpha, 0, 64)
    return solution + step * direction, residual - step * predicted


def run(function, outs, *args, keep=(), close=(), away=()):
    def kernel(*refs):
        values = [r if k in keep else r[...] for k, r in enumerate(refs[: len(args)])]
        results = function(*values)
        results = results if isinstance(results, tuple) else (results,)
        for ref, value in zip(refs[len(args) :], results, strict=True):
            ref[...] = value

    spaces = [pltpu.SMEM if a.dtype == jnp.int32 else pltpu.VMEM for a in args]
    args = [near(a) if k in close else a for k, a in enumerate(args)]
    outs = [s if isinstance(s, tuple) and isinstance(s[0], tuple) else (s, F32) for s in outs]
    got = pl.pallas_call(
        kernel,
        out_shape=[(pltpu.HBM if k in away else pltpu.VMEM)(s, d) for k, (s, d) in enumerate(outs)],
        in_specs=[pl.BlockSpec(memory_space=s) for s in spaces],
        out_specs=[pl.BlockSpec(memory_space=pltpu.VMEM) for _ in outs],
        compiler_params=pltpu.CompilerParams(vmem_limit_bytes=24 << 20),
    )(*args)
    return got if len(outs) > 1 else got[0]


def near(array):
    return pltpu.with_memory_space_constraint(array, pltpu.VMEM)


def far(array):
    return pltpu.with_memory_space_constraint(array, pltpu.HBM)


LIMIT = pltpu.CompilerParams(vmem_limit_bytes=24 << 20)
HBM, VMEM = pl.BlockSpec(memory_space=pltpu.HBM), pl.BlockSpec(memory_space=pltpu.VMEM)


def predict(direction, design, gradient_prev, whitening, residual):
    def kernel(direction, design, gradient_prev, whitening, residual, rows, rim, dir_v, des_v, old_v, rows_v, sems):
        def copy(source, target, k):
            copies.append(pltpu.make_async_copy(source, target, sems.at[k]))
            copies[-1].start()

        copies = []
        copy(direction, dir_v, 0)
        for i in range(4):
            copy(design.at[128 * i : 128 * i + 128], des_v.at[128 * i : 128 * i + 128], 1 + i)
        copy(gradient_prev, old_v, 5)
        copy(whitening.at[:BLOCK], rim.at[:BLOCK], 6)
        copy(residual.at[:, :BLOCK], rim.at[BLOCK:], 7)
        copies[0].wait()
        left = dir_v[...]
        for i in range(4):
            copies[1 + i].wait()
            part = times(left, split(des_v[128 * i : 128 * i + 128]), NT)
            for j in range(8):
                first = 9 * (4 * j + i)
                rows_v[first : first + 8] = part[8 * j : 8 * j + 8]
        copies[5].wait()
        old = row_squares(old_v[...])
        for m in range(32):
            rows_v[9 * m + 8 : 9 * m + 9] = old
        copy(rows_v, rows, 8)
        for k in range(6, 9):
            copies[k].wait()

    return pl.pallas_call(
        kernel,
        out_shape=[
            pltpu.HBM((9 * 32, 128), F32),
            pltpu.HBM((BLOCK + 64, BLOCK), F32),
        ],
        in_specs=[HBM] * 5,
        out_specs=[HBM] * 2,
        scratch_shapes=[
            pltpu.VMEM(direction.shape, F32),
            pltpu.VMEM(design.shape, F32),
            pltpu.VMEM(gradient_prev.shape, F32),
            pltpu.VMEM((9 * 32, 128), F32),
            pltpu.SemaphoreType.DMA((9,)),
        ],
        compiler_params=LIMIT,
        name="predict",
    )(*[far(a) for a in (direction, design, gradient_prev, whitening, residual)])


def banded(whitening, rim, residual, design):
    def kernel(rim, whitening, residual, design, b0, b1, b2, b3, back_grad, tap_v, res_v, des_v, sems):
        copies = [
            pltpu.make_async_copy(source, target, sems.at[k])
            for k, (source, target) in enumerate(((whitening, tap_v), (residual, res_v), (design, des_v)))
        ]
        for copy in copies:
            copy.start()
        for copy in copies[:2]:
            copy.wait()

        def fetched():
            copies[2].wait()
            return des_v[...]

        b0[...], b1[...], b2[...], b3[...], back_grad[...] = band(tap_v[...], rim[...], res_v[...], fetched)

    args = (whitening, residual, design)
    return pl.pallas_call(
        kernel,
        out_shape=[pltpu.VMEM((3, BLOCK, BLOCK), BF16)] * 4 + [pltpu.VMEM((64, design.shape[1]), F32)],
        in_specs=[VMEM] + [HBM] * 3,
        out_specs=[VMEM] * 5,
        scratch_shapes=[pltpu.VMEM(a.shape, F32) for a in args] + [pltpu.SemaphoreType.DMA((3,))],
        compiler_params=LIMIT,
        name="band",
    )(near(rim), *[far(a) for a in args])


def project(gathered, bands, back_grad, design):
    def kernel(gathered, b0, b1, b2, b3, back_grad, design, pieces, predicted, des_v, sem):
        copy = pltpu.make_async_copy(design, des_v, sem)
        copy.start()

        def fetched():
            copy.wait()
            return des_v[...]

        pieces[...], predicted[...] = whiten_and_project(
            gathered[...], b0[...], b1[...], b2[...], b3[...], back_grad[...], fetched
        )

    return pl.pallas_call(
        kernel,
        out_shape=[pltpu.VMEM((64, 2 * design.shape[1] + 128), F32), pltpu.VMEM((64, design.shape[0]), F32)],
        in_specs=[VMEM] * 6 + [HBM],
        out_specs=[VMEM] * 2,
        scratch_shapes=[pltpu.VMEM(design.shape, F32), pltpu.SemaphoreType.DMA],
        compiler_params=LIMIT,
        name="whiten_and_project",
    )(near(gathered), *[near(b) for b in bands], near(back_grad), far(design))


def exchange(rows, axis, groups=None):
    return lax.all_to_all(rows, axis, 0, 0, axis_index_groups=groups, tiled=True)


def per_device(design, whitening, solution, direction, gradient_prev, residual):
    blocks_t, blocks_c = lax.axis_size("tm"), lax.axis_size("coef")
    coefs = design.shape[1]
    solution, direction, gradient_prev, residual = solution.T, direction.T, gradient_prev.T, residual.T
    groups = [[4 * x + 2 * z + k for x in range(4) for k in range(2)] for z in range(2)]
    t = lax.axis_index("tm").astype(jnp.int32)
    place = (lax.shift_right_logical(t, 2) * 2 + (t & 1))[None]
    rows, rim = predict(direction, design, gradient_prev, whitening, residual)
    rows = exchange(rows.reshape(32, 9 * 128), "coef").reshape(9 * 32, 128)
    rim = lax.ppermute(rim, "tm", [(i + 1, i) for i in range(blocks_t - 1)])
    tile, old = run(collect, [(8, 128), (8, 128)], rows, close=(0,))
    pairs = []
    for t in range(blocks_t):
        for c in range(blocks_c):
            to = t + 1 if c % 4 >= 2 else t - 1
            if 0 <= to < blocks_t:
                pairs.append((t * blocks_c + c, to * blocks_c + c))
    rim_tile = lax.ppermute(tile, ("tm", "coef"), pairs)
    gathered = exchange(run(chunk, [(16 * 32, 128)], tile, rim_tile, close=(0, 1), away=(0,)), "coef")
    *bands, back_grad = banded(whitening, rim, residual, design)
    pieces, predicted = project(gathered, bands, back_grad, design)
    mine = run(sum_pieces, [(8, 2 * coefs + 128)], exchange(pieces, "tm", groups), close=(0,))
    other = lax.ppermute(mine, "tm", [(i, i ^ 2) for i in range(blocks_t)])
    grad, alpha, norms = run(
        step_piece, [(8, coefs), (8, 128), (32, 128)], place, mine, other, old, keep=(0,), close=(1, 2, 3)
    )
    norms = exchange(norms, "coef")
    new_solution, new_residual = run(
        update,
        [solution.shape, residual.shape],
        alpha,
        solution,
        direction,
        residual,
        predicted,
        close=(0, 4),
        away=(0, 1),
    )
    pieces = run(direction_piece, [(64, coefs)], place, norms, grad, old, direction, keep=(0, 4), close=(1, 2, 3), away=(0,))
    return new_solution.T, new_residual.T, exchange(pieces, "tm", groups).T


def solution(mesh):
    return jax.shard_map(
        per_device,
        mesh=mesh,
        in_specs=(
            P("tm", "coef"),
            P("tm", None),
            P("coef", None),
            P("coef", None),
            P("coef", None),
            P("tm", None),
        ),
        out_specs=(P("coef", None), P("tm", None), P("coef", None)),
        check_vma=False,
    )
```

```python
import jax
import jax.numpy as jnp
from jax import lax
from jax.experimental import pallas as pl
from jax.experimental.pallas import tpu as pltpu
from jax.sharding import PartitionSpec as P


BLOCK = 256
NN = (((1,), (0,)), ((), ()))
NT = (((1,), (1,)), ((), ()))
F32, BF16 = jnp.float32, jnp.bfloat16


def split(values):
    high = values.astype(BF16)
    return high, (values - high.astype(F32)).astype(BF16)


def times(left, right, dims):
    high, low = split(left)
    count = left.shape[0]
    first = lax.dot_general(jnp.concatenate([high, low], axis=0), right[0], dims, preferred_element_type=F32)
    return first[:count] + first[count:] + lax.dot_general(high, right[1], dims, preferred_element_type=F32)


def skew(rows):
    return pltpu.roll(rows, 0, 1, stride=1, stride_axis=0)


def as_row(column):
    shape = (column.shape[0], 128)
    pick = lax.broadcasted_iota(jnp.int32, shape, 0) == lax.broadcasted_iota(jnp.int32, shape, 1)
    return jnp.sum(jnp.where(pick, jnp.broadcast_to(column, shape), 0.0), axis=0, keepdims=True)


def row_squares(values):
    total = values[:, :128] * values[:, :128]
    for k in range(128, values.shape[1], 128):
        total = total + values[:, k : k + 128] * values[:, k : k + 128]
    return as_row(jnp.sum(total, axis=1, keepdims=True))


def as_column(row, first, count):
    shape = (count, 128)
    pick = lax.broadcasted_iota(jnp.int32, shape, 1) == lax.broadcasted_iota(jnp.int32, shape, 0) + first
    return jnp.sum(jnp.where(pick, jnp.broadcast_to(row[:1], shape), 0.0), axis=1, keepdims=True)


def collect(rows):
    tile, old = rows[:8], rows[8:9]
    for m in range(1, 32):
        tile = tile + rows[9 * m : 9 * m + 8]
        old = old + rows[9 * m + 8 : 9 * m + 9]
    return tile, jnp.broadcast_to(old, (8, 128))


def chunk(tile, rim):
    return jnp.concatenate([tile, rim] * 32, axis=0)


def band(whitening, rim, residual, design):
    taps = jnp.concatenate([whitening, rim[:BLOCK]], axis=0)
    lag = lax.broadcasted_iota(jnp.int32, (BLOCK, BLOCK), 0)
    lane = lax.broadcasted_iota(jnp.int32, (BLOCK, BLOCK), 1)
    mirror = jnp.where((lag + lane) % BLOCK == 0, 1.0, 0.0).astype(BF16)
    high, low = split(taps)
    least = (taps - high.astype(F32) - low.astype(F32)).astype(BF16)
    count = taps.shape[0]
    turned = lax.dot_general(jnp.concatenate([high, low, least], axis=0), mirror, NN, preferred_element_type=F32)
    turned = turned[:count] + turned[count : 2 * count] + turned[2 * count :]
    same, before = [], []
    for b in range(3):
        full = skew(turned[BLOCK * b : BLOCK * (b + 1)])
        same.append(split(jnp.where(lane <= lag, full, 0.0)))
        before.append(split(jnp.where(lane > lag, full, 0.0)))
    res = [residual[:, :BLOCK], residual[:, BLOCK:], rim[BLOCK:]]
    back = [times(res[b], same[b], NN) + times(res[b + 1], before[b + 1], NN) for b in range(2)]
    bands = [jnp.stack([m[k] for m in kind]) for kind in (same, before) for k in range(2)]
    return *bands, times(jnp.concatenate(back, axis=1), split(design()), NN)


def whiten_and_project(gathered, same_high, same_low, before_high, before_low, back_grad, design):
    def block(halves, row):
        return jnp.concatenate(
            [
                jnp.concatenate([gathered[16 * m + row : 16 * m + row + 8] for m in (4 * j + i for i in halves)], axis=1)
                for j in range(8)
            ],
            axis=0,
        )

    same = [(same_high[b], same_low[b]) for b in range(3)]
    before = [(before_high[b], before_low[b]) for b in range(3)]
    plain = [block((2, 3), 8), block((0, 1), 0), block((2, 3), 0), block((0, 1), 8)]
    pred = [times(plain[b + 1], same[b], NT) + times(plain[b], before[b], NT) for b in range(3)]
    own = jnp.concatenate(pred[:2], axis=1)
    energy = jnp.broadcast_to(row_squares(own), (64, 128))
    spread = [times(pred[b], same[b], NN) + times(pred[b + 1], before[b + 1], NN) for b in range(2)]
    grad = times(jnp.concatenate(spread, axis=1), split(design()), NN)
    return jnp.concatenate([back_grad, grad, energy], axis=1), own


def sum_pieces(pieces):
    total = pieces[:8]
    for m in range(1, 8):
        total = total + pieces[8 * m : 8 * m + 8]
    return total


def step_piece(place, mine, other, old):
    total = mine + other
    count = (total.shape[1] - 128) // 2
    alpha = old / total[:, 2 * count :]
    alpha = jnp.where(lax.broadcasted_iota(jnp.int32, alpha.shape, 1) < 64, alpha, 0.0)
    grad = total[:, :count] - as_column(alpha, 8 * place[0], 8) * total[:, count : 2 * count]
    return grad, alpha, jnp.broadcast_to(row_squares(grad), (32, 128))


def direction_piece(place, norms, grad, old, direction):
    norm = jnp.sum(norms, axis=0, keepdims=True)
    beta = as_column(norm, 0, 8) / as_column(old, 8 * place[0], 8)
    mine = direction[pl.ds(pl.multiple_of(8 * place[0], 8), 8), :]
    return jnp.concatenate([grad + beta * mine] * 8, axis=0)


def update(alpha, solution, direction, residual, predicted):
    step = as_column(alpha, 0, 64)
    return solution + step * direction, residual - step * predicted


def run(function, outs, *args, keep=(), close=(), away=()):
    def kernel(*refs):
        values = [r if k in keep else r[...] for k, r in enumerate(refs[: len(args)])]
        results = function(*values)
        results = results if isinstance(results, tuple) else (results,)
        for ref, value in zip(refs[len(args) :], results, strict=True):
            ref[...] = value

    spaces = [pltpu.SMEM if a.dtype == jnp.int32 else pltpu.VMEM for a in args]
    args = [near(a) if k in close else a for k, a in enumerate(args)]
    outs = [s if isinstance(s, tuple) and isinstance(s[0], tuple) else (s, F32) for s in outs]
    got = pl.pallas_call(
        kernel,
        out_shape=[(pltpu.HBM if k in away else pltpu.VMEM)(s, d) for k, (s, d) in enumerate(outs)],
        in_specs=[pl.BlockSpec(memory_space=s) for s in spaces],
        out_specs=[pl.BlockSpec(memory_space=pltpu.VMEM) for _ in outs],
        compiler_params=pltpu.CompilerParams(vmem_limit_bytes=24 << 20),
    )(*args)
    return got if len(outs) > 1 else got[0]


def near(array):
    return pltpu.with_memory_space_constraint(array, pltpu.VMEM)


def far(array):
    return pltpu.with_memory_space_constraint(array, pltpu.HBM)


LIMIT = pltpu.CompilerParams(vmem_limit_bytes=24 << 20)
HBM, VMEM = pl.BlockSpec(memory_space=pltpu.HBM), pl.BlockSpec(memory_space=pltpu.VMEM)


def predict(direction, design, gradient_prev, whitening, residual):
    def kernel(direction, design, gradient_prev, whitening, residual, rows, rim, dir_v, des_v, old_v, rows_v, sems):
        def copy(source, target, k):
            copies.append(pltpu.make_async_copy(source, target, sems.at[k]))
            copies[-1].start()

        copies = []
        copy(direction, dir_v, 0)
        for i in range(4):
            copy(design.at[128 * i : 128 * i + 128], des_v.at[128 * i : 128 * i + 128], 1 + i)
        copy(gradient_prev, old_v, 5)
        copy(whitening.at[:BLOCK], rim.at[:BLOCK], 6)
        copy(residual.at[:, :BLOCK], rim.at[BLOCK:], 7)
        copies[0].wait()
        left = dir_v[...]
        for i in range(4):
            copies[1 + i].wait()
            part = times(left, split(des_v[128 * i : 128 * i + 128]), NT)
            for j in range(8):
                first = 9 * (4 * j + i)
                rows_v[first : first + 8] = part[8 * j : 8 * j + 8]
        copies[5].wait()
        old = row_squares(old_v[...])
        for m in range(32):
            rows_v[9 * m + 8 : 9 * m + 9] = old
        copy(rows_v, rows, 8)
        for k in range(6, 9):
            copies[k].wait()

    return pl.pallas_call(
        kernel,
        out_shape=[
            pltpu.HBM((9 * 32, 128), F32),
            pltpu.VMEM((BLOCK + 64, BLOCK), F32),
        ],
        in_specs=[HBM] * 5,
        out_specs=[HBM, VMEM],
        scratch_shapes=[
            pltpu.VMEM(direction.shape, F32),
            pltpu.VMEM(design.shape, F32),
            pltpu.VMEM(gradient_prev.shape, F32),
            pltpu.VMEM((9 * 32, 128), F32),
            pltpu.SemaphoreType.DMA((9,)),
        ],
        compiler_params=LIMIT,
        name="predict",
    )(*[far(a) for a in (direction, design, gradient_prev, whitening, residual)])


def banded(whitening, rim, residual, design):
    def kernel(rim, whitening, residual, design, b0, b1, b2, b3, back_grad, tap_v, res_v, des_v, sems):
        copies = [
            pltpu.make_async_copy(source, target, sems.at[k])
            for k, (source, target) in enumerate(((whitening, tap_v), (residual, res_v), (design, des_v)))
        ]
        for copy in copies:
            copy.start()
        for copy in copies[:2]:
            copy.wait()

        def fetched():
            copies[2].wait()
            return des_v[...]

        b0[...], b1[...], b2[...], b3[...], back_grad[...] = band(tap_v[...], rim[...], res_v[...], fetched)

    args = (whitening, residual, design)
    return pl.pallas_call(
        kernel,
        out_shape=[pltpu.VMEM((3, BLOCK, BLOCK), BF16)] * 4 + [pltpu.VMEM((64, design.shape[1]), F32)],
        in_specs=[VMEM] + [HBM] * 3,
        out_specs=[VMEM] * 5,
        scratch_shapes=[pltpu.VMEM(a.shape, F32) for a in args] + [pltpu.SemaphoreType.DMA((3,))],
        compiler_params=LIMIT,
        name="band",
    )(near(rim), *[far(a) for a in args])


def project(gathered, bands, back_grad, design):
    def kernel(gathered, b0, b1, b2, b3, back_grad, design, pieces, predicted, des_v, sem):
        copy = pltpu.make_async_copy(design, des_v, sem)
        copy.start()

        def fetched():
            copy.wait()
            return des_v[...]

        pieces[...], predicted[...] = whiten_and_project(
            gathered[...], b0[...], b1[...], b2[...], b3[...], back_grad[...], fetched
        )

    return pl.pallas_call(
        kernel,
        out_shape=[pltpu.VMEM((64, 2 * design.shape[1] + 128), F32), pltpu.VMEM((64, design.shape[0]), F32)],
        in_specs=[VMEM] * 6 + [HBM],
        out_specs=[VMEM] * 2,
        scratch_shapes=[pltpu.VMEM(design.shape, F32), pltpu.SemaphoreType.DMA],
        compiler_params=LIMIT,
        name="whiten_and_project",
    )(near(gathered), *[near(b) for b in bands], near(back_grad), far(design))


def exchange(rows, axis, groups=None):
    return lax.all_to_all(rows, axis, 0, 0, axis_index_groups=groups, tiled=True)


def per_device(design, whitening, solution, direction, gradient_prev, residual):
    blocks_t, blocks_c = lax.axis_size("tm"), lax.axis_size("coef")
    coefs = design.shape[1]
    solution, direction, gradient_prev, residual = solution.T, direction.T, gradient_prev.T, residual.T
    groups = [[4 * x + 2 * z + k for x in range(4) for k in range(2)] for z in range(2)]
    t = lax.axis_index("tm").astype(jnp.int32)
    place = (lax.shift_right_logical(t, 2) * 2 + (t & 1))[None]
    rows, rim = predict(direction, design, gradient_prev, whitening, residual)
    rows = exchange(rows.reshape(32, 9 * 128), "coef").reshape(9 * 32, 128)
    rim = lax.ppermute(rim, "tm", [(i + 1, i) for i in range(blocks_t - 1)])
    *bands, back_grad = banded(whitening, rim, residual, design)
    tile, old = run(collect, [(8, 128), (8, 128)], rows, close=(0,))
    pairs = []
    for t in range(blocks_t):
        for c in range(blocks_c):
            to = t + 1 if c % 4 >= 2 else t - 1
            if 0 <= to < blocks_t:
                pairs.append((t * blocks_c + c, to * blocks_c + c))
    rim_tile = lax.ppermute(tile, ("tm", "coef"), pairs)
    gathered = exchange(run(chunk, [(16 * 32, 128)], tile, rim_tile, close=(0, 1)), "coef")
    pieces, predicted = project(gathered, bands, back_grad, design)
    mine = run(sum_pieces, [(8, 2 * coefs + 128)], exchange(pieces, "tm", groups), close=(0,))
    other = lax.ppermute(mine, "tm", [(i, i ^ 2) for i in range(blocks_t)])
    grad, alpha, norms = run(
        step_piece, [(8, coefs), (8, 128), (32, 128)], place, mine, other, old, keep=(0,), close=(1, 2, 3)
    )
    norms = exchange(norms, "coef")
    new_solution, new_residual = run(
        update,
        [solution.shape, residual.shape],
        alpha,
        solution,
        direction,
        residual,
        predicted,
        close=(0, 4),
        away=(0, 1),
    )
    pieces = run(direction_piece, [(64, coefs)], place, norms, grad, old, direction, keep=(0, 4), close=(1, 2, 3), away=(0,))
    return new_solution.T, new_residual.T, exchange(pieces, "tm", groups).T


def solution(mesh):
    return jax.shard_map(
        per_device,
        mesh=mesh,
        in_specs=(
            P("tm", "coef"),
            P("tm", None),
            P("coef", None),
            P("coef", None),
            P("coef", None),
            P("tm", None),
        ),
        out_specs=(P("coef", None), P("tm", None), P("coef", None)),
        check_vma=False,
    )
```

```python
import jax
import jax.numpy as jnp
from jax import lax
from jax.experimental import pallas as pl
from jax.experimental.pallas import tpu as pltpu
from jax.sharding import PartitionSpec as P


BLOCK = 256
NN = (((1,), (0,)), ((), ()))
NT = (((1,), (1,)), ((), ()))
F32, BF16 = jnp.float32, jnp.bfloat16


def split(values):
    high = values.astype(BF16)
    return high, (values - high.astype(F32)).astype(BF16)


def times(left, right, dims):
    high, low = split(left)
    count = left.shape[0]
    first = lax.dot_general(jnp.concatenate([high, low], axis=0), right[0], dims, preferred_element_type=F32)
    return first[:count] + first[count:] + lax.dot_general(high, right[1], dims, preferred_element_type=F32)


def skew(rows):
    return pltpu.roll(rows, 0, 1, stride=1, stride_axis=0)


def as_row(column):
    shape = (column.shape[0], 128)
    pick = lax.broadcasted_iota(jnp.int32, shape, 0) == lax.broadcasted_iota(jnp.int32, shape, 1)
    return jnp.sum(jnp.where(pick, jnp.broadcast_to(column, shape), 0.0), axis=0, keepdims=True)


def row_squares(values):
    total = values[:, :128] * values[:, :128]
    for k in range(128, values.shape[1], 128):
        total = total + values[:, k : k + 128] * values[:, k : k + 128]
    return as_row(jnp.sum(total, axis=1, keepdims=True))


def as_column(row, first, count):
    shape = (count, 128)
    pick = lax.broadcasted_iota(jnp.int32, shape, 1) == lax.broadcasted_iota(jnp.int32, shape, 0) + first
    return jnp.sum(jnp.where(pick, jnp.broadcast_to(row[:1], shape), 0.0), axis=1, keepdims=True)


def collect(rows):
    tile, old = rows[:8], rows[8:9]
    for m in range(1, 32):
        tile = tile + rows[9 * m : 9 * m + 8]
        old = old + rows[9 * m + 8 : 9 * m + 9]
    return tile, jnp.broadcast_to(old, (8, 128))


def chunk(tile, rim):
    return jnp.concatenate([tile, rim] * 32, axis=0)


def band(whitening, rim, residual, design):
    taps = jnp.concatenate([whitening, rim[:BLOCK]], axis=0)
    lag = lax.broadcasted_iota(jnp.int32, (BLOCK, BLOCK), 0)
    lane = lax.broadcasted_iota(jnp.int32, (BLOCK, BLOCK), 1)
    mirror = jnp.where((lag + lane) % BLOCK == 0, 1.0, 0.0).astype(BF16)
    high, low = split(taps)
    least = (taps - high.astype(F32) - low.astype(F32)).astype(BF16)
    count = taps.shape[0]
    turned = lax.dot_general(jnp.concatenate([high, low, least], axis=0), mirror, NN, preferred_element_type=F32)
    turned = turned[:count] + turned[count : 2 * count] + turned[2 * count :]
    same, before = [], []
    for b in range(3):
        full = skew(turned[BLOCK * b : BLOCK * (b + 1)])
        same.append(split(jnp.where(lane <= lag, full, 0.0)))
        before.append(split(jnp.where(lane > lag, full, 0.0)))
    res = [residual[:, :BLOCK], residual[:, BLOCK:], rim[BLOCK:]]
    back = [times(res[b], same[b], NN) + times(res[b + 1], before[b + 1], NN) for b in range(2)]
    bands = [jnp.stack([m[k] for m in kind]) for kind in (same, before) for k in range(2)]
    return *bands, times(jnp.concatenate(back, axis=1), split(design()), NN)


def whiten_and_project(gathered, same_high, same_low, before_high, before_low, back_grad, design):
    def block(halves, row):
        return jnp.concatenate(
            [
                jnp.concatenate([gathered[16 * m + row : 16 * m + row + 8] for m in (8 * i + j for i in halves)], axis=1)
                for j in range(8)
            ],
            axis=0,
        )

    same = [(same_high[b], same_low[b]) for b in range(3)]
    before = [(before_high[b], before_low[b]) for b in range(3)]
    plain = [block((2, 3), 8), block((0, 1), 0), block((2, 3), 0), block((0, 1), 8)]
    pred = [times(plain[b + 1], same[b], NT) + times(plain[b], before[b], NT) for b in range(3)]
    own = jnp.concatenate(pred[:2], axis=1)
    energy = jnp.broadcast_to(row_squares(own), (64, 128))
    spread = [times(pred[b], same[b], NN) + times(pred[b + 1], before[b + 1], NN) for b in range(2)]
    left = jnp.concatenate(spread, axis=1)
    parts = []
    for k in range(back_grad.shape[1] // BLOCK):
        parts.append(times(left, split(design(k)), NN))
    return jnp.concatenate([back_grad, *parts, energy], axis=1), own


def sum_pieces(pieces):
    total = pieces[:8]
    for m in range(1, 8):
        total = total + pieces[8 * m : 8 * m + 8]
    return total


def step_piece(place, mine, other, old):
    total = mine + other
    count = (total.shape[1] - 128) // 2
    alpha = old / total[:, 2 * count :]
    alpha = jnp.where(lax.broadcasted_iota(jnp.int32, alpha.shape, 1) < 64, alpha, 0.0)
    grad = total[:, :count] - as_column(alpha, 8 * place[0], 8) * total[:, count : 2 * count]
    return grad, alpha, jnp.broadcast_to(row_squares(grad), (32, 128))


def direction_piece(place, norms, grad, old, direction):
    norm = jnp.sum(norms, axis=0, keepdims=True)
    beta = as_column(norm, 0, 8) / as_column(old, 8 * place[0], 8)
    mine = direction[pl.ds(pl.multiple_of(8 * place[0], 8), 8), :]
    return jnp.concatenate([grad + beta * mine] * 8, axis=0)


def update(alpha, solution, direction, residual, predicted):
    step = as_column(alpha, 0, 64)
    return solution + step * direction, residual - step * predicted


def run(function, outs, *args, keep=(), close=(), away=()):
    def kernel(*refs):
        values = [r if k in keep else r[...] for k, r in enumerate(refs[: len(args)])]
        results = function(*values)
        results = results if isinstance(results, tuple) else (results,)
        for ref, value in zip(refs[len(args) :], results, strict=True):
            ref[...] = value

    spaces = [pltpu.SMEM if a.dtype == jnp.int32 else pltpu.VMEM for a in args]
    args = [near(a) if k in close else a for k, a in enumerate(args)]
    outs = [s if isinstance(s, tuple) and isinstance(s[0], tuple) else (s, F32) for s in outs]
    got = pl.pallas_call(
        kernel,
        out_shape=[(pltpu.HBM if k in away else pltpu.VMEM)(s, d) for k, (s, d) in enumerate(outs)],
        in_specs=[pl.BlockSpec(memory_space=s) for s in spaces],
        out_specs=[pl.BlockSpec(memory_space=pltpu.VMEM) for _ in outs],
        compiler_params=pltpu.CompilerParams(vmem_limit_bytes=24 << 20),
    )(*args)
    return got if len(outs) > 1 else got[0]


def near(array):
    return pltpu.with_memory_space_constraint(array, pltpu.VMEM)


def far(array):
    return pltpu.with_memory_space_constraint(array, pltpu.HBM)


LIMIT = pltpu.CompilerParams(vmem_limit_bytes=24 << 20)
HBM, VMEM = pl.BlockSpec(memory_space=pltpu.HBM), pl.BlockSpec(memory_space=pltpu.VMEM)


def predict(direction, design, gradient_prev, whitening, residual):
    def kernel(direction, design, gradient_prev, whitening, residual, rows, rim, dir_v, des_v, old_v, rows_v, sems):
        def copy(source, target, k):
            copies.append(pltpu.make_async_copy(source, target, sems.at[k]))
            copies[-1].start()

        copies = []
        copy(direction, dir_v, 0)
        copy(gradient_prev, old_v, 1)
        for i in range(4):
            copy(design.at[128 * i : 128 * i + 128], des_v.at[128 * i : 128 * i + 128], 2 + i)
        copy(whitening.at[:BLOCK], rim.at[:BLOCK], 6)
        copy(residual.at[:, :BLOCK], rim.at[BLOCK:], 7)
        copies[0].wait()
        left = dir_v[...]
        copies[1].wait()
        old = row_squares(old_v[...])
        for m in range(32):
            rows_v[9 * m + 8 : 9 * m + 9] = old
        for i in range(4):
            copies[2 + i].wait()
            part = times(left, split(des_v[128 * i : 128 * i + 128]), NT)
            for j in range(8):
                first = 9 * (8 * i + j)
                rows_v[first : first + 8] = part[8 * j : 8 * j + 8]
            copy(rows_v.at[72 * i : 72 * i + 72], rows.at[72 * i : 72 * i + 72], 8 + i)
        for k in range(6, 12):
            copies[k].wait()

    return pl.pallas_call(
        kernel,
        out_shape=[
            pltpu.HBM((9 * 32, 128), F32),
            pltpu.VMEM((BLOCK + 64, BLOCK), F32),
        ],
        in_specs=[HBM] * 5,
        out_specs=[HBM, VMEM],
        scratch_shapes=[
            pltpu.VMEM(direction.shape, F32),
            pltpu.VMEM(design.shape, F32),
            pltpu.VMEM(gradient_prev.shape, F32),
            pltpu.VMEM((9 * 32, 128), F32),
            pltpu.SemaphoreType.DMA((12,)),
        ],
        compiler_params=LIMIT,
        name="predict",
    )(*[far(a) for a in (direction, design, gradient_prev, whitening, residual)])


def banded(whitening, rim, residual, design):
    def kernel(rim, whitening, residual, design, b0, b1, b2, b3, back_grad, tap_v, res_v, des_v, sems):
        copies = [
            pltpu.make_async_copy(source, target, sems.at[k])
            for k, (source, target) in enumerate(((whitening, tap_v), (residual, res_v), (design, des_v)))
        ]
        for copy in copies:
            copy.start()
        for copy in copies[:2]:
            copy.wait()

        def fetched():
            copies[2].wait()
            return des_v[...]

        b0[...], b1[...], b2[...], b3[...], back_grad[...] = band(tap_v[...], rim[...], res_v[...], fetched)

    args = (whitening, residual, design)
    return pl.pallas_call(
        kernel,
        out_shape=[pltpu.VMEM((3, BLOCK, BLOCK), BF16)] * 4 + [pltpu.VMEM((64, design.shape[1]), F32)],
        in_specs=[VMEM] + [HBM] * 3,
        out_specs=[VMEM] * 5,
        scratch_shapes=[pltpu.VMEM(a.shape, F32) for a in args] + [pltpu.SemaphoreType.DMA((3,))],
        compiler_params=LIMIT,
        name="band",
    )(near(rim), *[far(a) for a in args])


def project(gathered, bands, back_grad, design):
    count = design.shape[1] // BLOCK

    def kernel(gathered, b0, b1, b2, b3, back_grad, design, pieces, predicted, des_v, sems):
        copies = []
        for k in range(count):
            cut = pl.ds(BLOCK * k, BLOCK)
            copies.append(pltpu.make_async_copy(design.at[:, cut], des_v.at[:, cut], sems.at[k]))
            copies[-1].start()

        def fetched(k):
            copies[k].wait()
            return des_v[:, BLOCK * k : BLOCK * (k + 1)]

        pieces[...], predicted[...] = whiten_and_project(
            gathered[...], b0[...], b1[...], b2[...], b3[...], back_grad[...], fetched
        )

    return pl.pallas_call(
        kernel,
        out_shape=[pltpu.VMEM((64, 2 * design.shape[1] + 128), F32), pltpu.VMEM((64, design.shape[0]), F32)],
        in_specs=[VMEM] * 6 + [HBM],
        out_specs=[VMEM] * 2,
        scratch_shapes=[pltpu.VMEM(design.shape, F32), pltpu.SemaphoreType.DMA((count,))],
        compiler_params=LIMIT,
        name="whiten_and_project",
    )(near(gathered), *[near(b) for b in bands], near(back_grad), far(design))


def exchange(rows, axis, groups=None):
    return lax.all_to_all(rows, axis, 0, 0, axis_index_groups=groups, tiled=True)


def per_device(design, whitening, solution, direction, gradient_prev, residual):
    blocks_t, blocks_c = lax.axis_size("tm"), lax.axis_size("coef")
    coefs = design.shape[1]
    solution, direction, gradient_prev, residual = solution.T, direction.T, gradient_prev.T, residual.T
    groups = [[4 * x + 2 * z + k for x in range(4) for k in range(2)] for z in range(2)]
    t = lax.axis_index("tm").astype(jnp.int32)
    place = (lax.shift_right_logical(t, 2) * 2 + (t & 1))[None]
    rows, rim = predict(direction, design, gradient_prev, whitening, residual)
    rows = exchange(rows.reshape(32, 9 * 128), "coef").reshape(9 * 32, 128)
    rim = lax.ppermute(rim, "tm", [(i + 1, i) for i in range(blocks_t - 1)])
    *bands, back_grad = banded(whitening, rim, residual, design)
    tile, old = run(collect, [(8, 128), (8, 128)], rows, close=(0,))
    pairs = []
    for t in range(blocks_t):
        for c in range(blocks_c):
            to = t + 1 if c >= blocks_c // 2 else t - 1
            if 0 <= to < blocks_t:
                pairs.append((t * blocks_c + c, to * blocks_c + c))
    rim_tile = lax.ppermute(tile, ("tm", "coef"), pairs)
    gathered = exchange(run(chunk, [(16 * 32, 128)], tile, rim_tile, close=(0, 1)), "coef")
    pieces, predicted = project(gathered, bands, back_grad, design)
    mine = run(sum_pieces, [(8, 2 * coefs + 128)], exchange(pieces, "tm", groups), close=(0,))
    other = lax.ppermute(mine, "tm", [(i, i ^ 2) for i in range(blocks_t)])
    grad, alpha, norms = run(
        step_piece, [(8, coefs), (8, 128), (32, 128)], place, mine, other, old, keep=(0,), close=(1, 2, 3), away=(2,)
    )
    norms = exchange(norms, "coef")
    new_solution, new_residual = run(
        update,
        [solution.shape, residual.shape],
        alpha,
        solution,
        direction,
        residual,
        predicted,
        close=(0, 4),
        away=(0, 1),
    )
    pieces = run(direction_piece, [(64, coefs)], place, norms, grad, old, direction, keep=(0, 4), close=(1, 2, 3))
    return new_solution.T, new_residual.T, exchange(pieces, "tm", groups).T


def solution(mesh):
    return jax.shard_map(
        per_device,
        mesh=mesh,
        in_specs=(
            P("tm", "coef"),
            P("tm", None),
            P("coef", None),
            P("coef", None),
            P("coef", None),
            P("tm", None),
        ),
        out_specs=(P("coef", None), P("tm", None), P("coef", None)),
        check_vma=False,
    )
```

```python
import jax
import jax.numpy as jnp
from jax import lax
from jax.experimental import pallas as pl
from jax.experimental.pallas import tpu as pltpu
from jax.sharding import PartitionSpec as P


BLOCK = 256
NN = (((1,), (0,)), ((), ()))
NT = (((1,), (1,)), ((), ()))
F32, BF16 = jnp.float32, jnp.bfloat16


def split(values):
    high = values.astype(BF16)
    return high, (values - high.astype(F32)).astype(BF16)


def times(left, right, dims):
    high, low = split(left)
    count = left.shape[0]
    first = lax.dot_general(jnp.concatenate([high, low], axis=0), right[0], dims, preferred_element_type=F32)
    return first[:count] + first[count:] + lax.dot_general(high, right[1], dims, preferred_element_type=F32)


def skew(rows):
    return pltpu.roll(rows, 0, 1, stride=1, stride_axis=0)


def as_row(column):
    shape = (column.shape[0], 128)
    pick = lax.broadcasted_iota(jnp.int32, shape, 0) == lax.broadcasted_iota(jnp.int32, shape, 1)
    return jnp.sum(jnp.where(pick, jnp.broadcast_to(column, shape), 0.0), axis=0, keepdims=True)


def row_squares(values):
    total = values[:, :128] * values[:, :128]
    for k in range(128, values.shape[1], 128):
        total = total + values[:, k : k + 128] * values[:, k : k + 128]
    return as_row(jnp.sum(total, axis=1, keepdims=True))


def as_column(row, first, count):
    shape = (count, 128)
    pick = lax.broadcasted_iota(jnp.int32, shape, 1) == lax.broadcasted_iota(jnp.int32, shape, 0) + first
    return jnp.sum(jnp.where(pick, jnp.broadcast_to(row[:1], shape), 0.0), axis=1, keepdims=True)


def collect(rows):
    tile, old = rows[:8], rows[8:9]
    for m in range(1, 32):
        tile = tile + rows[9 * m : 9 * m + 8]
        old = old + rows[9 * m + 8 : 9 * m + 9]
    return tile, jnp.broadcast_to(old, (8, 128))


def chunk(tile, rim):
    return jnp.concatenate([tile, rim] * 32, axis=0)


def band(whitening, rim, residual, design):
    taps = jnp.concatenate([whitening, rim[:BLOCK]], axis=0)
    lag = lax.broadcasted_iota(jnp.int32, (BLOCK, BLOCK), 0)
    lane = lax.broadcasted_iota(jnp.int32, (BLOCK, BLOCK), 1)
    mirror = jnp.where((lag + lane) % BLOCK == 0, 1.0, 0.0).astype(BF16)
    high, low = split(taps)
    least = (taps - high.astype(F32) - low.astype(F32)).astype(BF16)
    count = taps.shape[0]
    turned = lax.dot_general(jnp.concatenate([high, low, least], axis=0), mirror, NN, preferred_element_type=F32)
    turned = turned[:count] + turned[count : 2 * count] + turned[2 * count :]
    same, before = [], []
    for b in range(3):
        full = skew(turned[BLOCK * b : BLOCK * (b + 1)])
        same.append(split(jnp.where(lane <= lag, full, 0.0)))
        before.append(split(jnp.where(lane > lag, full, 0.0)))
    res = [residual[:, :BLOCK], residual[:, BLOCK:], rim[BLOCK:]]
    back = [times(res[b], same[b], NN) + times(res[b + 1], before[b + 1], NN) for b in range(2)]
    bands = [jnp.stack([m[k] for m in kind]) for kind in (same, before) for k in range(2)]
    return *bands, times(jnp.concatenate(back, axis=1), split(design()), NN)


def whiten_and_project(gathered, same_high, same_low, before_high, before_low, back_grad, design):
    def block(halves, row):
        return jnp.concatenate(
            [
                jnp.concatenate([gathered[16 * m + row : 16 * m + row + 8] for m in (8 * i + j for i in halves)], axis=1)
                for j in range(8)
            ],
            axis=0,
        )

    same = [(same_high[b], same_low[b]) for b in range(3)]
    before = [(before_high[b], before_low[b]) for b in range(3)]
    plain = [block((2, 3), 8), block((0, 1), 0), block((2, 3), 0), block((0, 1), 8)]
    pred = [times(plain[b + 1], same[b], NT) + times(plain[b], before[b], NT) for b in range(3)]
    own = jnp.concatenate(pred[:2], axis=1)
    energy = jnp.broadcast_to(row_squares(own), (64, 128))
    spread = [times(pred[b], same[b], NN) + times(pred[b + 1], before[b + 1], NN) for b in range(2)]
    left = jnp.concatenate(spread, axis=1)
    parts = []
    for k in range(back_grad.shape[1] // BLOCK):
        parts.append(times(left, split(design(k)), NN))
    return jnp.concatenate([back_grad, *parts, energy], axis=1), own


def sum_pieces(pieces):
    total = pieces[:8]
    for m in range(1, 8):
        total = total + pieces[8 * m : 8 * m + 8]
    return total


def step_piece(place, mine, other, old):
    total = mine + other
    count = (total.shape[1] - 128) // 2
    alpha = old / total[:, 2 * count :]
    alpha = jnp.where(lax.broadcasted_iota(jnp.int32, alpha.shape, 1) < 64, alpha, 0.0)
    grad = total[:, :count] - as_column(alpha, 8 * place[0], 8) * total[:, count : 2 * count]
    return grad, alpha, jnp.broadcast_to(row_squares(grad), (32, 128))


def direction_piece(place, norms, grad, old, direction):
    norm = jnp.sum(norms, axis=0, keepdims=True)
    beta = as_column(norm, 0, 8) / as_column(old, 8 * place[0], 8)
    mine = direction[pl.ds(pl.multiple_of(8 * place[0], 8), 8), :]
    return jnp.concatenate([grad + beta * mine] * 8, axis=0)


def update(alpha, solution, direction, residual, predicted):
    step = as_column(alpha, 0, 64)
    return solution + step * direction, residual - step * predicted


def run(function, outs, *args, keep=(), close=(), away=()):
    def kernel(*refs):
        values = [r if k in keep else r[...] for k, r in enumerate(refs[: len(args)])]
        results = function(*values)
        results = results if isinstance(results, tuple) else (results,)
        for ref, value in zip(refs[len(args) :], results, strict=True):
            ref[...] = value

    spaces = [pltpu.SMEM if a.dtype == jnp.int32 else pltpu.VMEM for a in args]
    args = [near(a) if k in close else a for k, a in enumerate(args)]
    outs = [s if isinstance(s, tuple) and isinstance(s[0], tuple) else (s, F32) for s in outs]
    got = pl.pallas_call(
        kernel,
        out_shape=[(pltpu.HBM if k in away else pltpu.VMEM)(s, d) for k, (s, d) in enumerate(outs)],
        in_specs=[pl.BlockSpec(memory_space=s) for s in spaces],
        out_specs=[pl.BlockSpec(memory_space=pltpu.VMEM) for _ in outs],
        compiler_params=pltpu.CompilerParams(vmem_limit_bytes=24 << 20),
    )(*args)
    return got if len(outs) > 1 else got[0]


def near(array):
    return pltpu.with_memory_space_constraint(array, pltpu.VMEM)


def far(array):
    return pltpu.with_memory_space_constraint(array, pltpu.HBM)


LIMIT = pltpu.CompilerParams(vmem_limit_bytes=24 << 20)
HBM, VMEM = pl.BlockSpec(memory_space=pltpu.HBM), pl.BlockSpec(memory_space=pltpu.VMEM)


def predict(direction, design, gradient_prev):
    def kernel(direction, design, gradient_prev, rows, dir_v, des_v, old_v, rows_v, sems):
        def copy(source, target, k):
            copies.append(pltpu.make_async_copy(source, target, sems.at[k]))
            copies[-1].start()

        copies = []
        copy(direction, dir_v, 0)
        copy(gradient_prev, old_v, 1)
        for i in range(4):
            copy(design.at[128 * i : 128 * i + 128], des_v.at[128 * i : 128 * i + 128], 2 + i)
        copies[0].wait()
        left = dir_v[...]
        copies[1].wait()
        old = row_squares(old_v[...])
        for m in range(32):
            rows_v[9 * m + 8 : 9 * m + 9] = old
        for i in range(4):
            copies[2 + i].wait()
            part = times(left, split(des_v[128 * i : 128 * i + 128]), NT)
            for j in range(8):
                first = 9 * (8 * i + j)
                rows_v[first : first + 8] = part[8 * j : 8 * j + 8]
            copy(rows_v.at[72 * i : 72 * i + 72], rows.at[72 * i : 72 * i + 72], 6 + i)
        for k in range(6, 10):
            copies[k].wait()

    return pl.pallas_call(
        kernel,
        out_shape=pltpu.HBM((9 * 32, 128), F32),
        in_specs=[HBM] * 3,
        out_specs=HBM,
        scratch_shapes=[
            pltpu.VMEM(direction.shape, F32),
            pltpu.VMEM(design.shape, F32),
            pltpu.VMEM(gradient_prev.shape, F32),
            pltpu.VMEM((9 * 32, 128), F32),
            pltpu.SemaphoreType.DMA((10,)),
        ],
        compiler_params=LIMIT,
        name="predict",
    )(far(direction), far(design), far(gradient_prev))


def rim_rows(whitening, residual):
    def kernel(whitening, residual, rim, sems):
        copies = [
            pltpu.make_async_copy(whitening.at[:BLOCK], rim.at[:BLOCK], sems.at[0]),
            pltpu.make_async_copy(residual.at[:, :BLOCK], rim.at[BLOCK:], sems.at[1]),
        ]
        for copy in copies:
            copy.start()
        for copy in copies:
            copy.wait()

    return pl.pallas_call(
        kernel,
        out_shape=pltpu.VMEM((BLOCK + 64, BLOCK), F32),
        in_specs=[HBM] * 2,
        out_specs=VMEM,
        scratch_shapes=[pltpu.SemaphoreType.DMA((2,))],
        compiler_params=LIMIT,
        name="rim_rows",
    )(far(whitening), far(residual))


def banded(whitening, rim, residual, design):
    def kernel(rim, whitening, residual, design, b0, b1, b2, b3, back_grad, tap_v, res_v, des_v, sems):
        copies = [
            pltpu.make_async_copy(source, target, sems.at[k])
            for k, (source, target) in enumerate(((whitening, tap_v), (residual, res_v), (design, des_v)))
        ]
        for copy in copies:
            copy.start()
        for copy in copies[:2]:
            copy.wait()

        def fetched():
            copies[2].wait()
            return des_v[...]

        b0[...], b1[...], b2[...], b3[...], back_grad[...] = band(tap_v[...], rim[...], res_v[...], fetched)

    args = (whitening, residual, design)
    return pl.pallas_call(
        kernel,
        out_shape=[pltpu.VMEM((3, BLOCK, BLOCK), BF16)] * 4 + [pltpu.VMEM((64, design.shape[1]), F32)],
        in_specs=[VMEM] + [HBM] * 3,
        out_specs=[VMEM] * 5,
        scratch_shapes=[pltpu.VMEM(a.shape, F32) for a in args] + [pltpu.SemaphoreType.DMA((3,))],
        compiler_params=LIMIT,
        name="band",
    )(near(rim), *[far(a) for a in args])


def project(gathered, bands, back_grad, design):
    count = design.shape[1] // BLOCK

    def kernel(gathered, b0, b1, b2, b3, back_grad, design, pieces, predicted, des_v, sems):
        copies = []
        for k in range(count):
            cut = pl.ds(BLOCK * k, BLOCK)
            copies.append(pltpu.make_async_copy(design.at[:, cut], des_v.at[:, cut], sems.at[k]))
            copies[-1].start()

        def fetched(k):
            copies[k].wait()
            return des_v[:, BLOCK * k : BLOCK * (k + 1)]

        pieces[...], predicted[...] = whiten_and_project(
            gathered[...], b0[...], b1[...], b2[...], b3[...], back_grad[...], fetched
        )

    return pl.pallas_call(
        kernel,
        out_shape=[pltpu.VMEM((64, 2 * design.shape[1] + 128), F32), pltpu.VMEM((64, design.shape[0]), F32)],
        in_specs=[VMEM] * 6 + [HBM],
        out_specs=[VMEM] * 2,
        scratch_shapes=[pltpu.VMEM(design.shape, F32), pltpu.SemaphoreType.DMA((count,))],
        compiler_params=LIMIT,
        name="whiten_and_project",
    )(near(gathered), *[near(b) for b in bands], near(back_grad), far(design))


def exchange(rows, axis, groups=None):
    return lax.all_to_all(rows, axis, 0, 0, axis_index_groups=groups, tiled=True)


def per_device(design, whitening, solution, direction, gradient_prev, residual):
    blocks_t, blocks_c = lax.axis_size("tm"), lax.axis_size("coef")
    coefs = design.shape[1]
    solution, direction, gradient_prev, residual = solution.T, direction.T, gradient_prev.T, residual.T
    groups = [[4 * x + 2 * z + k for x in range(4) for k in range(2)] for z in range(2)]
    t = lax.axis_index("tm").astype(jnp.int32)
    place = (lax.shift_right_logical(t, 2) * 2 + (t & 1))[None]
    rim = lax.ppermute(rim_rows(whitening, residual), "tm", [(i + 1, i) for i in range(blocks_t - 1)])
    rows = predict(direction, design, gradient_prev)
    rows = exchange(rows.reshape(32, 9 * 128), "coef").reshape(9 * 32, 128)
    *bands, back_grad = banded(whitening, rim, residual, design)
    tile, old = run(collect, [(8, 128), (8, 128)], rows, close=(0,))
    pairs = []
    for t in range(blocks_t):
        for c in range(blocks_c):
            to = t + 1 if c >= blocks_c // 2 else t - 1
            if 0 <= to < blocks_t:
                pairs.append((t * blocks_c + c, to * blocks_c + c))
    rim_tile = lax.ppermute(tile, ("tm", "coef"), pairs)
    gathered = exchange(run(chunk, [(16 * 32, 128)], tile, rim_tile, close=(0, 1)), "coef")
    pieces, predicted = project(gathered, bands, back_grad, design)
    mine = run(sum_pieces, [(8, 2 * coefs + 128)], exchange(pieces, "tm", groups), close=(0,))
    other = lax.ppermute(mine, "tm", [(i, i ^ 2) for i in range(blocks_t)])
    grad, alpha, norms = run(
        step_piece, [(8, coefs), (8, 128), (32, 128)], place, mine, other, old, keep=(0,), close=(1, 2, 3), away=(2,)
    )
    norms = exchange(norms, "coef")
    new_solution, new_residual = run(
        update,
        [solution.shape, residual.shape],
        alpha,
        solution,
        direction,
        residual,
        predicted,
        close=(0, 4),
        away=(0, 1),
    )
    pieces = run(direction_piece, [(64, coefs)], place, norms, grad, old, direction, keep=(0, 4), close=(1, 2, 3))
    return new_solution.T, new_residual.T, exchange(pieces, "tm", groups).T


def solution(mesh):
    return jax.shard_map(
        per_device,
        mesh=mesh,
        in_specs=(
            P("tm", "coef"),
            P("tm", None),
            P("coef", None),
            P("coef", None),
            P("coef", None),
            P("tm", None),
        ),
        out_specs=(P("coef", None), P("tm", None), P("coef", None)),
        check_vma=False,
    )
```

```python
import jax
import jax.numpy as jnp
from jax import lax
from jax.experimental import pallas as pl
from jax.experimental.pallas import tpu as pltpu
from jax.sharding import PartitionSpec as P


BLOCK = 256
NN = (((1,), (0,)), ((), ()))
NT = (((1,), (1,)), ((), ()))
F32, BF16 = jnp.float32, jnp.bfloat16


def split(values):
    high = values.astype(BF16)
    return high, (values - high.astype(F32)).astype(BF16)


def times(left, right, dims):
    high, low = split(left)
    count = left.shape[0]
    first = lax.dot_general(jnp.concatenate([high, low], axis=0), right[0], dims, preferred_element_type=F32)
    return first[:count] + first[count:] + lax.dot_general(high, right[1], dims, preferred_element_type=F32)


def skew(rows):
    return pltpu.roll(rows, 0, 1, stride=1, stride_axis=0)


def as_row(column):
    shape = (column.shape[0], 128)
    pick = lax.broadcasted_iota(jnp.int32, shape, 0) == lax.broadcasted_iota(jnp.int32, shape, 1)
    return jnp.sum(jnp.where(pick, jnp.broadcast_to(column, shape), 0.0), axis=0, keepdims=True)


def row_squares(values):
    total = values[:, :128] * values[:, :128]
    for k in range(128, values.shape[1], 128):
        total = total + values[:, k : k + 128] * values[:, k : k + 128]
    return as_row(jnp.sum(total, axis=1, keepdims=True))


def as_column(row, first, count):
    shape = (count, 128)
    pick = lax.broadcasted_iota(jnp.int32, shape, 1) == lax.broadcasted_iota(jnp.int32, shape, 0) + first
    return jnp.sum(jnp.where(pick, jnp.broadcast_to(row[:1], shape), 0.0), axis=1, keepdims=True)


def collect(rows):
    tile, old = rows[:8], rows[8:9]
    for m in range(1, 32):
        tile = tile + rows[9 * m : 9 * m + 8]
        old = old + rows[9 * m + 8 : 9 * m + 9]
    return tile, jnp.broadcast_to(old, (8, 128))


def chunk(tile, rim):
    return jnp.concatenate([tile, rim] * 32, axis=0)


def band(whitening, rim, residual, design):
    taps = jnp.concatenate([whitening, rim[:BLOCK]], axis=0)
    lag = lax.broadcasted_iota(jnp.int32, (BLOCK, BLOCK), 0)
    lane = lax.broadcasted_iota(jnp.int32, (BLOCK, BLOCK), 1)
    mirror = jnp.where((lag + lane) % BLOCK == 0, 1.0, 0.0).astype(BF16)
    high, low = split(taps)
    least = (taps - high.astype(F32) - low.astype(F32)).astype(BF16)
    count = taps.shape[0]
    turned = lax.dot_general(jnp.concatenate([high, low, least], axis=0), mirror, NN, preferred_element_type=F32)
    turned = turned[:count] + turned[count : 2 * count] + turned[2 * count :]
    same, before = [], []
    for b in range(3):
        full = skew(turned[BLOCK * b : BLOCK * (b + 1)])
        same.append(split(jnp.where(lane <= lag, full, 0.0)))
        before.append(split(jnp.where(lane > lag, full, 0.0)))
    res = [residual[:, :BLOCK], residual[:, BLOCK:], rim[BLOCK:]]
    back = [times(res[b], same[b], NN) + times(res[b + 1], before[b + 1], NN) for b in range(2)]
    bands = [jnp.stack([m[k] for m in kind]) for kind in (same, before) for k in range(2)]
    return *bands, times(jnp.concatenate(back, axis=1), split(design()), NN)


def whiten_and_project(odd, gathered, same_high, same_low, before_high, before_low, back_grad, design):
    def block(halves, row, swap=0):
        return jnp.concatenate(
            [
                jnp.concatenate([gathered[16 * m + row : 16 * m + row + 8] for m in (8 * i + (j ^ swap) for i in halves)], axis=1)
                for j in range(8)
            ],
            axis=0,
        )

    same = [(same_high[b], same_low[b]) for b in range(3)]
    before = [(before_high[b], before_low[b]) for b in range(3)]
    plain = [
        jnp.where(odd, block((2, 3), 8), block((2, 3), 8, 2)),
        block((0, 1), 0),
        block((2, 3), 0),
        jnp.where(odd, block((0, 1), 8, 2), block((0, 1), 8)),
    ]
    pred = [times(plain[b + 1], same[b], NT) + times(plain[b], before[b], NT) for b in range(3)]
    own = jnp.concatenate(pred[:2], axis=1)
    energy = jnp.broadcast_to(row_squares(own), (64, 128))
    spread = [times(pred[b], same[b], NN) + times(pred[b + 1], before[b + 1], NN) for b in range(2)]
    left = jnp.concatenate(spread, axis=1)
    parts = []
    for k in range(back_grad.shape[1] // BLOCK):
        parts.append(times(left, split(design(k)), NN))
    return jnp.concatenate([back_grad, *parts, energy], axis=1), own


def sum_pieces(pieces):
    total = pieces[:8]
    for m in range(1, 8):
        total = total + pieces[8 * m : 8 * m + 8]
    return total


def own_group(place):
    return (lax.shift_right_logical(place[0], 2) * 2 + (place[0] & 1)) * 8


def step_piece(place, mine, other, old):
    total = mine + other
    count = (total.shape[1] - 128) // 2
    alpha = old / total[:, 2 * count :]
    alpha = jnp.where(lax.broadcasted_iota(jnp.int32, alpha.shape, 1) < 64, alpha, 0.0)
    grad = total[:, :count] - as_column(alpha, own_group(place), 8) * total[:, count : 2 * count]
    return grad, alpha, jnp.broadcast_to(row_squares(grad), (32, 128))


def direction_piece(place, norms, grad, old, direction):
    norm = jnp.sum(norms, axis=0, keepdims=True)
    beta = as_column(norm, 0, 8) / as_column(old, own_group(place), 8)
    mine = direction[pl.ds(pl.multiple_of(own_group(place), 8), 8), :]
    return jnp.concatenate([grad + beta * mine] * 8, axis=0)


def update(alpha, solution, direction, residual, predicted):
    step = as_column(alpha, 0, 64)
    return solution + step * direction, residual - step * predicted


def run(function, outs, *args, keep=(), close=(), away=()):
    def kernel(*refs):
        values = [r if k in keep else r[...] for k, r in enumerate(refs[: len(args)])]
        results = function(*values)
        results = results if isinstance(results, tuple) else (results,)
        for ref, value in zip(refs[len(args) :], results, strict=True):
            ref[...] = value

    spaces = [pltpu.SMEM if a.dtype == jnp.int32 else pltpu.VMEM for a in args]
    args = [near(a) if k in close else a for k, a in enumerate(args)]
    outs = [s if isinstance(s, tuple) and isinstance(s[0], tuple) else (s, F32) for s in outs]
    got = pl.pallas_call(
        kernel,
        out_shape=[(pltpu.HBM if k in away else pltpu.VMEM)(s, d) for k, (s, d) in enumerate(outs)],
        in_specs=[pl.BlockSpec(memory_space=s) for s in spaces],
        out_specs=[pl.BlockSpec(memory_space=pltpu.VMEM) for _ in outs],
        compiler_params=pltpu.CompilerParams(vmem_limit_bytes=24 << 20),
    )(*args)
    return got if len(outs) > 1 else got[0]


def near(array):
    return pltpu.with_memory_space_constraint(array, pltpu.VMEM)


def far(array):
    return pltpu.with_memory_space_constraint(array, pltpu.HBM)


LIMIT = pltpu.CompilerParams(vmem_limit_bytes=24 << 20)
HBM, VMEM = pl.BlockSpec(memory_space=pltpu.HBM), pl.BlockSpec(memory_space=pltpu.VMEM)


def predict(direction, design, gradient_prev, whitening, residual):
    def kernel(direction, design, gradient_prev, whitening, residual, rows, rim, dir_v, des_v, old_v, rows_v, sems):
        def copy(source, target, k):
            copies.append(pltpu.make_async_copy(source, target, sems.at[k]))
            copies[-1].start()

        copies = []
        copy(direction, dir_v, 0)
        copy(gradient_prev, old_v, 1)
        for i in range(4):
            copy(design.at[128 * i : 128 * i + 128], des_v.at[128 * i : 128 * i + 128], 2 + i)
        copy(whitening.at[:BLOCK], rim.at[:BLOCK], 6)
        copy(residual.at[:, :BLOCK], rim.at[BLOCK:], 7)
        copies[0].wait()
        left = dir_v[...]
        copies[1].wait()
        old = row_squares(old_v[...])
        for m in range(32):
            rows_v[9 * m + 8 : 9 * m + 9] = old
        for i in range(4):
            copies[2 + i].wait()
            part = times(left, split(des_v[128 * i : 128 * i + 128]), NT)
            for j in range(8):
                first = 9 * (8 * i + j)
                rows_v[first : first + 8] = part[8 * j : 8 * j + 8]
            copy(rows_v.at[72 * i : 72 * i + 72], rows.at[72 * i : 72 * i + 72], 8 + i)
        for k in range(6, 12):
            copies[k].wait()

    return pl.pallas_call(
        kernel,
        out_shape=[
            pltpu.HBM((9 * 32, 128), F32),
            pltpu.VMEM((BLOCK + 64, BLOCK), F32),
        ],
        in_specs=[HBM] * 5,
        out_specs=[HBM, VMEM],
        scratch_shapes=[
            pltpu.VMEM(direction.shape, F32),
            pltpu.VMEM(design.shape, F32),
            pltpu.VMEM(gradient_prev.shape, F32),
            pltpu.VMEM((9 * 32, 128), F32),
            pltpu.SemaphoreType.DMA((12,)),
        ],
        compiler_params=LIMIT,
        name="predict",
    )(*[far(a) for a in (direction, design, gradient_prev, whitening, residual)])


def banded(place, whitening, rim, residual, design):
    def kernel(place, rim, whitening, residual, design, b0, b1, b2, b3, back_grad, tap_v, res_v, des_v, sems):
        copies = [
            pltpu.make_async_copy(source, target, sems.at[k])
            for k, (source, target) in enumerate(((whitening, tap_v), (residual, res_v), (design, des_v)))
        ]
        for copy in copies:
            copy.start()
        for copy in copies[:2]:
            copy.wait()

        def fetched():
            copies[2].wait()
            return des_v[...]

        b0[...], b1[...], b2[...], b3[...], back_grad[...] = band(tap_v[...], rim[...], res_v[...], fetched)

    args = (whitening, residual, design)
    return pl.pallas_call(
        kernel,
        out_shape=[pltpu.VMEM((3, BLOCK, BLOCK), BF16)] * 4 + [pltpu.VMEM((64, design.shape[1]), F32)],
        in_specs=[pl.BlockSpec(memory_space=pltpu.SMEM), VMEM] + [HBM] * 3,
        out_specs=[VMEM] * 5,
        scratch_shapes=[pltpu.VMEM(a.shape, F32) for a in args] + [pltpu.SemaphoreType.DMA((3,))],
        compiler_params=LIMIT,
        name="band",
    )(place, near(rim), *[far(a) for a in args])


def project(place, gathered, bands, back_grad, design):
    count = design.shape[1] // BLOCK

    def kernel(place, gathered, b0, b1, b2, b3, back_grad, design, pieces, predicted, des_v, sems):
        copies = []
        for k in range(count):
            cut = pl.ds(BLOCK * k, BLOCK)
            copies.append(pltpu.make_async_copy(design.at[:, cut], des_v.at[:, cut], sems.at[k]))
            copies[-1].start()

        def fetched(k):
            copies[k].wait()
            return des_v[:, BLOCK * k : BLOCK * (k + 1)]

        pieces[...], predicted[...] = whiten_and_project(
            (place[0] & 1) == 1, gathered[...], b0[...], b1[...], b2[...], b3[...], back_grad[...], fetched
        )

    return pl.pallas_call(
        kernel,
        out_shape=[pltpu.VMEM((64, 2 * design.shape[1] + 128), F32), pltpu.VMEM((64, design.shape[0]), F32)],
        in_specs=[pl.BlockSpec(memory_space=pltpu.SMEM)] + [VMEM] * 6 + [HBM],
        out_specs=[VMEM] * 2,
        scratch_shapes=[pltpu.VMEM(design.shape, F32), pltpu.SemaphoreType.DMA((count,))],
        compiler_params=LIMIT,
        name="whiten_and_project",
    )(place, near(gathered), *[near(b) for b in bands], near(back_grad), far(design))


def exchange(rows, axis, groups=None):
    return lax.all_to_all(rows, axis, 0, 0, axis_index_groups=groups, tiled=True)


def neighbours(blocks_t, blocks_c, step):
    pairs = []
    for t in range(blocks_t):
        for c in range(blocks_c):
            to = t + step(c)
            if 0 <= to < blocks_t:
                pairs.append((t * blocks_c + c, to * blocks_c + (c if t // 2 == to // 2 else c ^ 2)))
    return pairs


def per_device(design, whitening, solution, direction, gradient_prev, residual):
    blocks_t, blocks_c = lax.axis_size("tm"), lax.axis_size("coef")
    coefs = design.shape[1]
    solution, direction, gradient_prev, residual = solution.T, direction.T, gradient_prev.T, residual.T
    groups = [[4 * x + 2 * z + k for x in range(4) for k in range(2)] for z in range(2)]
    t = lax.axis_index("tm").astype(jnp.int32)
    place = t[None]
    rows, rim = predict(direction, design, gradient_prev, whitening, residual)
    rows = exchange(rows.reshape(32, 9 * 128), "coef").reshape(9 * 32, 128)
    rim = lax.ppermute(rim, ("tm", "coef"), neighbours(blocks_t, blocks_c, lambda c: -1))
    *bands, back_grad = banded(place, whitening, rim, residual, design)
    tile, old = run(collect, [(8, 128), (8, 128)], rows, close=(0,))
    rim_tile = lax.ppermute(
        tile, ("tm", "coef"), neighbours(blocks_t, blocks_c, lambda c: 1 if c >= blocks_c // 2 else -1)
    )
    gathered = exchange(run(chunk, [(16 * 32, 128)], tile, rim_tile, close=(0, 1), away=(0,)), "coef")
    pieces, predicted = project(place, gathered, bands, back_grad, design)
    mine = run(sum_pieces, [(8, 2 * coefs + 128)], exchange(pieces, "tm", groups), close=(0,))
    other = lax.ppermute(mine, "tm", [(i, i ^ 2) for i in range(blocks_t)])
    grad, alpha, norms = run(
        step_piece, [(8, coefs), (8, 128), (32, 128)], place, mine, other, old, keep=(0,), close=(1, 2, 3), away=(2,)
    )
    norms = exchange(norms, "coef")
    new_solution, new_residual = run(
        update,
        [solution.shape, residual.shape],
        alpha,
        solution,
        direction,
        residual,
        predicted,
        close=(0, 4),
        away=(0, 1),
    )
    pieces = run(direction_piece, [(64, coefs)], place, norms, grad, old, direction, keep=(0, 4), close=(1, 2, 3))
    return new_solution.T, new_residual.T, exchange(pieces, "tm", groups).T


def solution(mesh):
    return jax.shard_map(
        per_device,
        mesh=mesh,
        in_specs=(
            P("tm", "coef"),
            P("tm", None),
            P("coef", None),
            P("coef", None),
            P("coef", None),
            P("tm", None),
        ),
        out_specs=(P("coef", None), P("tm", None), P("coef", None)),
        check_vma=False,
    )
```

```python
import jax
import jax.numpy as jnp
from jax import lax
from jax.experimental import pallas as pl
from jax.experimental.pallas import tpu as pltpu
from jax.sharding import PartitionSpec as P


BLOCK = 256
NN = (((1,), (0,)), ((), ()))
NT = (((1,), (1,)), ((), ()))
F32, BF16 = jnp.float32, jnp.bfloat16


def split(values):
    high = values.astype(BF16)
    return high, (values - high.astype(F32)).astype(BF16)


def times(left, right, dims):
    high, low = split(left)
    count = left.shape[0]
    first = lax.dot_general(jnp.concatenate([high, low], axis=0), right[0], dims, preferred_element_type=F32)
    return first[:count] + first[count:] + lax.dot_general(high, right[1], dims, preferred_element_type=F32)


def skew(rows):
    return pltpu.roll(rows, 0, 1, stride=1, stride_axis=0)


def as_row(column):
    shape = (column.shape[0], 128)
    pick = lax.broadcasted_iota(jnp.int32, shape, 0) == lax.broadcasted_iota(jnp.int32, shape, 1)
    return jnp.sum(jnp.where(pick, jnp.broadcast_to(column, shape), 0.0), axis=0, keepdims=True)


def row_squares(values):
    total = values[:, :128] * values[:, :128]
    for k in range(128, values.shape[1], 128):
        total = total + values[:, k : k + 128] * values[:, k : k + 128]
    return as_row(jnp.sum(total, axis=1, keepdims=True))


def as_column(row, first, count):
    shape = (count, 128)
    pick = lax.broadcasted_iota(jnp.int32, shape, 1) == lax.broadcasted_iota(jnp.int32, shape, 0) + first
    return jnp.sum(jnp.where(pick, jnp.broadcast_to(row[:1], shape), 0.0), axis=1, keepdims=True)


def collect(rows):
    tile, old = rows[:8], rows[8:9]
    for m in range(1, 32):
        tile = tile + rows[9 * m : 9 * m + 8]
        old = old + rows[9 * m + 8 : 9 * m + 9]
    return tile, jnp.broadcast_to(old, (8, 128))


def chunk(tile, rim):
    return jnp.concatenate([tile, rim] * 32, axis=0)


def band(whitening, rim, residual, design):
    taps = jnp.concatenate([whitening, rim[:BLOCK]], axis=0)
    lag = lax.broadcasted_iota(jnp.int32, (BLOCK, BLOCK), 0)
    lane = lax.broadcasted_iota(jnp.int32, (BLOCK, BLOCK), 1)
    mirror = jnp.where((lag + lane) % BLOCK == 0, 1.0, 0.0).astype(BF16)
    high, low = split(taps)
    least = (taps - high.astype(F32) - low.astype(F32)).astype(BF16)
    count = taps.shape[0]
    turned = lax.dot_general(jnp.concatenate([high, low, least], axis=0), mirror, NN, preferred_element_type=F32)
    turned = turned[:count] + turned[count : 2 * count] + turned[2 * count :]
    same, before = [], []
    for b in range(3):
        full = skew(turned[BLOCK * b : BLOCK * (b + 1)])
        same.append(split(jnp.where(lane <= lag, full, 0.0)))
        before.append(split(jnp.where(lane > lag, full, 0.0)))
    res = [residual[:, :BLOCK], residual[:, BLOCK:], rim[BLOCK:]]
    back = [times(res[b], same[b], NN) + times(res[b + 1], before[b + 1], NN) for b in range(2)]
    bands = [jnp.stack([m[k] for m in kind]) for kind in (same, before) for k in range(2)]
    return *bands, times(jnp.concatenate(back, axis=1), split(design()), NN)


def whiten_and_project(odd, gathered, same_high, same_low, before_high, before_low, keep, got, design):
    def block(halves, row, swap=0):
        return jnp.concatenate(
            [
                jnp.concatenate([gathered[16 * m + row : 16 * m + row + 8] for m in (8 * i + (j ^ swap) for i in halves)], axis=1)
                for j in range(8)
            ],
            axis=0,
        )

    same = [(same_high[b], same_low[b]) for b in range(3)]
    before = [(before_high[b], before_low[b]) for b in range(3)]
    plain = [
        jnp.where(odd, block((2, 3), 8), block((2, 3), 8, 2)),
        block((0, 1), 0),
        block((2, 3), 0),
        jnp.where(odd, block((0, 1), 8, 2), block((0, 1), 8)),
    ]
    pred = [times(plain[b + 1], same[b], NT) + times(plain[b], before[b], NT) for b in range(3)]
    own = jnp.concatenate(pred[:2], axis=1)
    energy = jnp.broadcast_to(row_squares(own), (64, 128))
    spread = [times(pred[b], same[b], NN) + times(pred[b + 1], before[b + 1], NN) for b in range(2)]
    left = jnp.concatenate(spread, axis=1)
    parts = []
    for k in range(2 * keep.shape[1] // BLOCK):
        parts.append(times(left, split(design(k)), NN))
    return jnp.concatenate([keep + got, *parts, energy], axis=1), own


def sum_pieces(pieces):
    total = pieces[:8]
    for m in range(1, 8):
        total = total + pieces[8 * m : 8 * m + 8]
    return total


def upper(place):
    return (place[0] & 2) == 2


def halves_of(values, swap):
    half = values.shape[1] // 2
    first, second = values[:, :half], values[:, half:]
    return jnp.where(swap, second, first), jnp.where(swap, first, second)


def own_group(place):
    return (lax.shift_right_logical(place[0], 2) * 2 + (place[0] & 1)) * 8


def step_piece(place, mine, other, old):
    half = (mine.shape[1] - 128) // 3
    back = jnp.concatenate([mine[:, :half], other[:, :half]], axis=1)
    back = jnp.concatenate(halves_of(back, upper(place)), axis=1)
    total = mine[:, half:] + other[:, half:]
    alpha = old / total[:, 2 * half :]
    alpha = jnp.where(lax.broadcasted_iota(jnp.int32, alpha.shape, 1) < 64, alpha, 0.0)
    grad = back - as_column(alpha, own_group(place), 8) * total[:, : 2 * half]
    return grad, alpha, jnp.broadcast_to(row_squares(grad), (32, 128))


def direction_piece(place, norms, grad, old, direction):
    norm = jnp.sum(norms, axis=0, keepdims=True)
    beta = as_column(norm, 0, 8) / as_column(old, own_group(place), 8)
    mine = direction[pl.ds(pl.multiple_of(own_group(place), 8), 8), :]
    return jnp.concatenate([grad + beta * mine] * 8, axis=0)


def update(alpha, solution, direction, residual, predicted):
    step = as_column(alpha, 0, 64)
    return solution + step * direction, residual - step * predicted


def run(function, outs, *args, keep=(), close=(), away=()):
    def kernel(*refs):
        values = [r if k in keep else r[...] for k, r in enumerate(refs[: len(args)])]
        results = function(*values)
        results = results if isinstance(results, tuple) else (results,)
        for ref, value in zip(refs[len(args) :], results, strict=True):
            ref[...] = value

    spaces = [pltpu.SMEM if a.dtype == jnp.int32 else pltpu.VMEM for a in args]
    args = [near(a) if k in close else a for k, a in enumerate(args)]
    outs = [s if isinstance(s, tuple) and isinstance(s[0], tuple) else (s, F32) for s in outs]
    got = pl.pallas_call(
        kernel,
        out_shape=[(pltpu.HBM if k in away else pltpu.VMEM)(s, d) for k, (s, d) in enumerate(outs)],
        in_specs=[pl.BlockSpec(memory_space=s) for s in spaces],
        out_specs=[pl.BlockSpec(memory_space=pltpu.VMEM) for _ in outs],
        compiler_params=pltpu.CompilerParams(vmem_limit_bytes=24 << 20),
    )(*args)
    return got if len(outs) > 1 else got[0]


def near(array):
    return pltpu.with_memory_space_constraint(array, pltpu.VMEM)


def far(array):
    return pltpu.with_memory_space_constraint(array, pltpu.HBM)


LIMIT = pltpu.CompilerParams(vmem_limit_bytes=24 << 20)
HBM, VMEM = pl.BlockSpec(memory_space=pltpu.HBM), pl.BlockSpec(memory_space=pltpu.VMEM)


def predict(direction, design, gradient_prev, whitening, residual):
    def kernel(direction, design, gradient_prev, whitening, residual, rows, rim, dir_v, des_v, old_v, rows_v, sems):
        def copy(source, target, k):
            copies.append(pltpu.make_async_copy(source, target, sems.at[k]))
            copies[-1].start()

        copies = []
        copy(direction, dir_v, 0)
        copy(gradient_prev, old_v, 1)
        for i in range(4):
            copy(design.at[128 * i : 128 * i + 128], des_v.at[128 * i : 128 * i + 128], 2 + i)
        copy(whitening.at[:BLOCK], rim.at[:BLOCK], 6)
        copy(residual.at[:, :BLOCK], rim.at[BLOCK:], 7)
        copies[0].wait()
        left = dir_v[...]
        copies[1].wait()
        old = row_squares(old_v[...])
        for m in range(32):
            rows_v[9 * m + 8 : 9 * m + 9] = old
        for i in range(4):
            copies[2 + i].wait()
            part = times(left, split(des_v[128 * i : 128 * i + 128]), NT)
            for j in range(8):
                first = 9 * (8 * i + j)
                rows_v[first : first + 8] = part[8 * j : 8 * j + 8]
            copy(rows_v.at[72 * i : 72 * i + 72], rows.at[72 * i : 72 * i + 72], 8 + i)
        for k in range(6, 12):
            copies[k].wait()

    return pl.pallas_call(
        kernel,
        out_shape=[
            pltpu.HBM((9 * 32, 128), F32),
            pltpu.VMEM((BLOCK + 64, BLOCK), F32),
        ],
        in_specs=[HBM] * 5,
        out_specs=[HBM, VMEM],
        scratch_shapes=[
            pltpu.VMEM(direction.shape, F32),
            pltpu.VMEM(design.shape, F32),
            pltpu.VMEM(gradient_prev.shape, F32),
            pltpu.VMEM((9 * 32, 128), F32),
            pltpu.SemaphoreType.DMA((12,)),
        ],
        compiler_params=LIMIT,
        name="predict",
    )(*[far(a) for a in (direction, design, gradient_prev, whitening, residual)])


def banded(place, whitening, rim, residual, design):
    def kernel(place, rim, whitening, residual, design, b0, b1, b2, b3, keep, send, tap_v, res_v, des_v, sems):
        copies = [
            pltpu.make_async_copy(source, target, sems.at[k])
            for k, (source, target) in enumerate(((whitening, tap_v), (residual, res_v), (design, des_v)))
        ]
        for copy in copies:
            copy.start()
        for copy in copies[:2]:
            copy.wait()

        def fetched():
            copies[2].wait()
            return des_v[...]

        b0[...], b1[...], b2[...], b3[...], back = band(tap_v[...], rim[...], res_v[...], fetched)
        keep[...], send[...] = halves_of(back, upper(place))

    args = (whitening, residual, design)
    return pl.pallas_call(
        kernel,
        out_shape=[pltpu.VMEM((3, BLOCK, BLOCK), BF16)] * 4 + [pltpu.VMEM((64, design.shape[1] // 2), F32)] * 2,
        in_specs=[pl.BlockSpec(memory_space=pltpu.SMEM), VMEM] + [HBM] * 3,
        out_specs=[VMEM] * 6,
        scratch_shapes=[pltpu.VMEM(a.shape, F32) for a in args] + [pltpu.SemaphoreType.DMA((3,))],
        compiler_params=LIMIT,
        name="band",
    )(place, near(rim), *[far(a) for a in args])


def project(place, gathered, bands, keep, got, design):
    count = design.shape[1] // BLOCK

    def kernel(place, gathered, b0, b1, b2, b3, keep, got, design, pieces, predicted, des_v, sems):
        copies = []
        for k in range(count):
            cut = pl.ds(BLOCK * k, BLOCK)
            copies.append(pltpu.make_async_copy(design.at[:, cut], des_v.at[:, cut], sems.at[k]))
            copies[-1].start()

        def fetched(k):
            copies[k].wait()
            return des_v[:, BLOCK * k : BLOCK * (k + 1)]

        pieces[...], predicted[...] = whiten_and_project(
            (place[0] & 1) == 1, gathered[...], b0[...], b1[...], b2[...], b3[...], keep[...], got[...], fetched
        )

    return pl.pallas_call(
        kernel,
        out_shape=[pltpu.VMEM((64, design.shape[1] // 2 * 3 + 128), F32), pltpu.VMEM((64, design.shape[0]), F32)],
        in_specs=[pl.BlockSpec(memory_space=pltpu.SMEM)] + [VMEM] * 7 + [HBM],
        out_specs=[VMEM] * 2,
        scratch_shapes=[pltpu.VMEM(design.shape, F32), pltpu.SemaphoreType.DMA((count,))],
        compiler_params=LIMIT,
        name="whiten_and_project",
    )(place, near(gathered), *[near(b) for b in bands], near(keep), near(got), far(design))


def exchange(rows, axis, groups=None):
    return lax.all_to_all(rows, axis, 0, 0, axis_index_groups=groups, tiled=True)


def neighbours(blocks_t, blocks_c, step):
    pairs = []
    for t in range(blocks_t):
        for c in range(blocks_c):
            to = t + step(c)
            if 0 <= to < blocks_t:
                pairs.append((t * blocks_c + c, to * blocks_c + (c if t // 2 == to // 2 else c ^ 2)))
    return pairs


def per_device(design, whitening, solution, direction, gradient_prev, residual):
    blocks_t, blocks_c = lax.axis_size("tm"), lax.axis_size("coef")
    coefs = design.shape[1]
    solution, direction, gradient_prev, residual = solution.T, direction.T, gradient_prev.T, residual.T
    groups = [[4 * x + 2 * z + k for x in range(4) for k in range(2)] for z in range(2)]
    t = lax.axis_index("tm").astype(jnp.int32)
    place = t[None]
    rows, rim = predict(direction, design, gradient_prev, whitening, residual)
    rows = exchange(rows.reshape(32, 9 * 128), "coef").reshape(9 * 32, 128)
    rim = lax.ppermute(rim, ("tm", "coef"), neighbours(blocks_t, blocks_c, lambda c: -1))
    *bands, keep, send = banded(place, whitening, rim, residual, design)
    tile, old = run(collect, [(8, 128), (8, 128)], rows, close=(0,))
    rim_tile = lax.ppermute(
        tile, ("tm", "coef"), neighbours(blocks_t, blocks_c, lambda c: 1 if c >= blocks_c // 2 else -1)
    )
    gathered = exchange(run(chunk, [(16 * 32, 128)], tile, rim_tile, close=(0, 1), away=(0,)), "coef")
    across = [(i, i ^ 2) for i in range(blocks_t)]
    got = lax.ppermute(send, "tm", across)
    pieces, predicted = project(place, gathered, bands, keep, got, design)
    mine = run(sum_pieces, [(8, coefs // 2 * 3 + 128)], exchange(pieces, "tm", groups), close=(0,))
    other = lax.ppermute(mine, "tm", across)
    grad, alpha, norms = run(
        step_piece, [(8, coefs), (8, 128), (32, 128)], place, mine, other, old, keep=(0,), close=(1, 2, 3), away=(2,)
    )
    norms = exchange(norms, "coef")
    new_solution, new_residual = run(
        update,
        [solution.shape, residual.shape],
        alpha,
        solution,
        direction,
        residual,
        predicted,
        close=(0, 4),
        away=(0, 1),
    )
    pieces = run(direction_piece, [(64, coefs)], place, norms, grad, old, direction, keep=(0, 4), close=(1, 2, 3))
    return new_solution.T, new_residual.T, exchange(pieces, "tm", groups).T


def solution(mesh):
    return jax.shard_map(
        per_device,
        mesh=mesh,
        in_specs=(
            P("tm", "coef"),
            P("tm", None),
            P("coef", None),
            P("coef", None),
            P("coef", None),
            P("tm", None),
        ),
        out_specs=(P("coef", None), P("tm", None), P("coef", None)),
        check_vma=False,
    )
```

```python
import jax
import jax.numpy as jnp
from jax import lax
from jax.experimental import pallas as pl
from jax.experimental.pallas import tpu as pltpu
from jax.sharding import PartitionSpec as P


BLOCK = 256
NN = (((1,), (0,)), ((), ()))
NT = (((1,), (1,)), ((), ()))
F32, BF16 = jnp.float32, jnp.bfloat16


def split(values):
    high = values.astype(BF16)
    return high, (values - high.astype(F32)).astype(BF16)


def times(left, right, dims):
    high, low = split(left)
    count = left.shape[0]
    first = lax.dot_general(jnp.concatenate([high, low], axis=0), right[0], dims, preferred_element_type=F32)
    return first[:count] + first[count:] + lax.dot_general(high, right[1], dims, preferred_element_type=F32)


def skew(rows):
    return pltpu.roll(rows, 0, 1, stride=1, stride_axis=0)


def as_row(column):
    shape = (column.shape[0], 128)
    pick = lax.broadcasted_iota(jnp.int32, shape, 0) == lax.broadcasted_iota(jnp.int32, shape, 1)
    return jnp.sum(jnp.where(pick, jnp.broadcast_to(column, shape), 0.0), axis=0, keepdims=True)


def row_squares(values):
    total = values[:, :128] * values[:, :128]
    for k in range(128, values.shape[1], 128):
        total = total + values[:, k : k + 128] * values[:, k : k + 128]
    return as_row(jnp.sum(total, axis=1, keepdims=True))


def as_column(row, first, count):
    shape = (count, 128)
    pick = lax.broadcasted_iota(jnp.int32, shape, 1) == lax.broadcasted_iota(jnp.int32, shape, 0) + first
    return jnp.sum(jnp.where(pick, jnp.broadcast_to(row[:1], shape), 0.0), axis=1, keepdims=True)


def collect(rows):
    tile, old = rows[:8], rows[8:9]
    for m in range(1, 32):
        tile = tile + rows[9 * m : 9 * m + 8]
        old = old + rows[9 * m + 8 : 9 * m + 9]
    return tile, jnp.broadcast_to(old, (8, 128))


def chunk(tile, rim):
    return jnp.concatenate([tile, rim] * 32, axis=0)


def band(whitening, rim, residual, design):
    taps = jnp.concatenate([whitening, rim[:BLOCK]], axis=0)
    lag = lax.broadcasted_iota(jnp.int32, (BLOCK, BLOCK), 0)
    lane = lax.broadcasted_iota(jnp.int32, (BLOCK, BLOCK), 1)
    mirror = jnp.where((lag + lane) % BLOCK == 0, 1.0, 0.0).astype(BF16)
    high, low = split(taps)
    least = (taps - high.astype(F32) - low.astype(F32)).astype(BF16)
    count = taps.shape[0]
    turned = lax.dot_general(jnp.concatenate([high, low, least], axis=0), mirror, NN, preferred_element_type=F32)
    turned = turned[:count] + turned[count : 2 * count] + turned[2 * count :]
    same, before = [], []
    for b in range(3):
        full = skew(turned[BLOCK * b : BLOCK * (b + 1)])
        same.append(split(jnp.where(lane <= lag, full, 0.0)))
        before.append(split(jnp.where(lane > lag, full, 0.0)))
    res = [residual[:, :BLOCK], residual[:, BLOCK:], rim[BLOCK:]]
    back = [times(res[b], same[b], NN) + times(res[b + 1], before[b + 1], NN) for b in range(2)]
    bands = [jnp.stack([m[k] for m in kind]) for kind in (same, before) for k in range(2)]
    return *bands, times(jnp.concatenate(back, axis=1), split(design()), NN)


def whiten_and_project(odd, gathered, same_high, same_low, before_high, before_low, keep, got, design):
    def block(halves, row, swap=0):
        return jnp.concatenate(
            [
                jnp.concatenate([gathered[16 * m + row : 16 * m + row + 8] for m in (8 * i + (j ^ swap) for i in halves)], axis=1)
                for j in range(8)
            ],
            axis=0,
        )

    same = [(same_high[b], same_low[b]) for b in range(3)]
    before = [(before_high[b], before_low[b]) for b in range(3)]
    plain = [
        jnp.where(odd, block((2, 3), 8), block((2, 3), 8, 2)),
        block((0, 1), 0),
        block((2, 3), 0),
        jnp.where(odd, block((0, 1), 8, 2), block((0, 1), 8)),
    ]
    pred = [times(plain[b + 1], same[b], NT) + times(plain[b], before[b], NT) for b in range(3)]
    own = jnp.concatenate(pred[:2], axis=1)
    energy = jnp.broadcast_to(row_squares(own), (64, 128))
    spread = [times(pred[b], same[b], NN) + times(pred[b + 1], before[b + 1], NN) for b in range(2)]
    left = jnp.concatenate(spread, axis=1)
    parts = []
    for k in range(2 * keep.shape[1] // BLOCK):
        parts.append(times(left, split(design(k)), NN))
    return jnp.concatenate([keep + got, *parts, energy], axis=1), own


def sum_pieces(pieces):
    half = (pieces.shape[1] - 128) // 3
    part = [pieces[8 * m : 8 * m + 8] for m in range(8)]
    back = [part[k][:, :half] + part[k + 2][:, :half] + part[k + 4][:, :half] + part[k + 6][:, :half] for k in range(2)]
    total = part[0][:, half:]
    for m in range(1, 8):
        total = total + part[m][:, half:]
    return jnp.concatenate([*back, total], axis=1)


def upper(place):
    return (place[0] & 1) == 1


def halves_of(values, swap):
    half = values.shape[1] // 2
    first, second = values[:, :half], values[:, half:]
    return jnp.where(swap, second, first), jnp.where(swap, first, second)


def own_group(place):
    return (lax.shift_right_logical(place[0], 2) * 2 + (place[0] & 1)) * 8


def step_piece(place, mine, other, old):
    total = mine + other
    count = (total.shape[1] - 128) // 2
    alpha = old / total[:, 2 * count :]
    alpha = jnp.where(lax.broadcasted_iota(jnp.int32, alpha.shape, 1) < 64, alpha, 0.0)
    grad = total[:, :count] - as_column(alpha, own_group(place), 8) * total[:, count : 2 * count]
    return grad, alpha, jnp.broadcast_to(row_squares(grad), (32, 128))


def direction_piece(place, norms, grad, old, direction):
    norm = jnp.sum(norms, axis=0, keepdims=True)
    beta = as_column(norm, 0, 8) / as_column(old, own_group(place), 8)
    mine = direction[pl.ds(pl.multiple_of(own_group(place), 8), 8), :]
    return jnp.concatenate([grad + beta * mine] * 8, axis=0)


def update(alpha, solution, direction, residual, predicted):
    step = as_column(alpha, 0, 64)
    return solution + step * direction, residual - step * predicted


def run(function, outs, *args, keep=(), close=(), away=()):
    def kernel(*refs):
        values = [r if k in keep else r[...] for k, r in enumerate(refs[: len(args)])]
        results = function(*values)
        results = results if isinstance(results, tuple) else (results,)
        for ref, value in zip(refs[len(args) :], results, strict=True):
            ref[...] = value

    spaces = [pltpu.SMEM if a.dtype == jnp.int32 else pltpu.VMEM for a in args]
    args = [near(a) if k in close else a for k, a in enumerate(args)]
    outs = [s if isinstance(s, tuple) and isinstance(s[0], tuple) else (s, F32) for s in outs]
    got = pl.pallas_call(
        kernel,
        out_shape=[(pltpu.HBM if k in away else pltpu.VMEM)(s, d) for k, (s, d) in enumerate(outs)],
        in_specs=[pl.BlockSpec(memory_space=s) for s in spaces],
        out_specs=[pl.BlockSpec(memory_space=pltpu.VMEM) for _ in outs],
        compiler_params=pltpu.CompilerParams(vmem_limit_bytes=24 << 20),
    )(*args)
    return got if len(outs) > 1 else got[0]


def near(array):
    return pltpu.with_memory_space_constraint(array, pltpu.VMEM)


def far(array):
    return pltpu.with_memory_space_constraint(array, pltpu.HBM)


LIMIT = pltpu.CompilerParams(vmem_limit_bytes=24 << 20)
HBM, VMEM = pl.BlockSpec(memory_space=pltpu.HBM), pl.BlockSpec(memory_space=pltpu.VMEM)


def predict(direction, design, gradient_prev, whitening, residual):
    def kernel(direction, design, gradient_prev, whitening, residual, rows, rim, dir_v, des_v, old_v, rows_v, sems):
        def copy(source, target, k):
            copies.append(pltpu.make_async_copy(source, target, sems.at[k]))
            copies[-1].start()

        copies = []
        copy(direction, dir_v, 0)
        copy(gradient_prev, old_v, 1)
        for i in range(4):
            copy(design.at[128 * i : 128 * i + 128], des_v.at[128 * i : 128 * i + 128], 2 + i)
        copy(whitening.at[:BLOCK], rim.at[:BLOCK], 6)
        copy(residual.at[:, :BLOCK], rim.at[BLOCK:], 7)
        copies[0].wait()
        left = dir_v[...]
        copies[1].wait()
        old = row_squares(old_v[...])
        for m in range(32):
            rows_v[9 * m + 8 : 9 * m + 9] = old
        for i in range(4):
            copies[2 + i].wait()
            part = times(left, split(des_v[128 * i : 128 * i + 128]), NT)
            for j in range(8):
                first = 9 * (8 * i + j)
                rows_v[first : first + 8] = part[8 * j : 8 * j + 8]
            copy(rows_v.at[72 * i : 72 * i + 72], rows.at[72 * i : 72 * i + 72], 8 + i)
        for k in range(6, 12):
            copies[k].wait()

    return pl.pallas_call(
        kernel,
        out_shape=[
            pltpu.HBM((9 * 32, 128), F32),
            pltpu.VMEM((BLOCK + 64, BLOCK), F32),
        ],
        in_specs=[HBM] * 5,
        out_specs=[HBM, VMEM],
        scratch_shapes=[
            pltpu.VMEM(direction.shape, F32),
            pltpu.VMEM(design.shape, F32),
            pltpu.VMEM(gradient_prev.shape, F32),
            pltpu.VMEM((9 * 32, 128), F32),
            pltpu.SemaphoreType.DMA((12,)),
        ],
        compiler_params=LIMIT,
        name="predict",
    )(*[far(a) for a in (direction, design, gradient_prev, whitening, residual)])


def banded(place, whitening, rim, residual, design):
    def kernel(place, rim, whitening, residual, design, b0, b1, b2, b3, keep, send, tap_v, res_v, des_v, sems):
        copies = [
            pltpu.make_async_copy(source, target, sems.at[k])
            for k, (source, target) in enumerate(((whitening, tap_v), (residual, res_v), (design, des_v)))
        ]
        for copy in copies:
            copy.start()
        for copy in copies[:2]:
            copy.wait()

        def fetched():
            copies[2].wait()
            return des_v[...]

        b0[...], b1[...], b2[...], b3[...], back = band(tap_v[...], rim[...], res_v[...], fetched)
        keep[...], send[...] = halves_of(back, upper(place))

    args = (whitening, residual, design)
    return pl.pallas_call(
        kernel,
        out_shape=[pltpu.VMEM((3, BLOCK, BLOCK), BF16)] * 4 + [pltpu.VMEM((64, design.shape[1] // 2), F32)] * 2,
        in_specs=[pl.BlockSpec(memory_space=pltpu.SMEM), VMEM] + [HBM] * 3,
        out_specs=[VMEM] * 6,
        scratch_shapes=[pltpu.VMEM(a.shape, F32) for a in args] + [pltpu.SemaphoreType.DMA((3,))],
        compiler_params=LIMIT,
        name="band",
    )(place, near(rim), *[far(a) for a in args])


def project(place, gathered, bands, keep, got, design):
    count = design.shape[1] // BLOCK

    def kernel(place, gathered, b0, b1, b2, b3, keep, got, design, pieces, predicted, des_v, sems):
        copies = []
        for k in range(count):
            cut = pl.ds(BLOCK * k, BLOCK)
            copies.append(pltpu.make_async_copy(design.at[:, cut], des_v.at[:, cut], sems.at[k]))
            copies[-1].start()

        def fetched(k):
            copies[k].wait()
            return des_v[:, BLOCK * k : BLOCK * (k + 1)]

        pieces[...], predicted[...] = whiten_and_project(
            (place[0] & 1) == 1, gathered[...], b0[...], b1[...], b2[...], b3[...], keep[...], got[...], fetched
        )

    return pl.pallas_call(
        kernel,
        out_shape=[pltpu.VMEM((64, design.shape[1] // 2 * 3 + 128), F32), pltpu.VMEM((64, design.shape[0]), F32)],
        in_specs=[pl.BlockSpec(memory_space=pltpu.SMEM)] + [VMEM] * 7 + [HBM],
        out_specs=[VMEM] * 2,
        scratch_shapes=[pltpu.VMEM(design.shape, F32), pltpu.SemaphoreType.DMA((count,))],
        compiler_params=LIMIT,
        name="whiten_and_project",
    )(place, near(gathered), *[near(b) for b in bands], near(keep), near(got), far(design))


def exchange(rows, axis, groups=None):
    return lax.all_to_all(rows, axis, 0, 0, axis_index_groups=groups, tiled=True)


def neighbours(blocks_t, blocks_c, step):
    pairs = []
    for t in range(blocks_t):
        for c in range(blocks_c):
            to = t + step(c)
            if 0 <= to < blocks_t:
                pairs.append((t * blocks_c + c, to * blocks_c + (c if t // 2 == to // 2 else c ^ 2)))
    return pairs


def per_device(design, whitening, solution, direction, gradient_prev, residual):
    blocks_t, blocks_c = lax.axis_size("tm"), lax.axis_size("coef")
    coefs = design.shape[1]
    solution, direction, gradient_prev, residual = solution.T, direction.T, gradient_prev.T, residual.T
    groups = [[4 * x + 2 * z + k for x in range(4) for k in range(2)] for z in range(2)]
    t = lax.axis_index("tm").astype(jnp.int32)
    place = t[None]
    rows, rim = predict(direction, design, gradient_prev, whitening, residual)
    rows = exchange(rows.reshape(32, 9 * 128), "coef").reshape(9 * 32, 128)
    rim = lax.ppermute(rim, ("tm", "coef"), neighbours(blocks_t, blocks_c, lambda c: -1))
    *bands, keep, send = banded(place, whitening, rim, residual, design)
    tile, old = run(collect, [(8, 128), (8, 128)], rows, close=(0,))
    rim_tile = lax.ppermute(
        tile, ("tm", "coef"), neighbours(blocks_t, blocks_c, lambda c: 1 if c >= blocks_c // 2 else -1)
    )
    gathered = exchange(run(chunk, [(16 * 32, 128)], tile, rim_tile, close=(0, 1), away=(0,)), "coef")
    got = lax.ppermute(send, "tm", [(i, i ^ 1) for i in range(blocks_t)])
    pieces, predicted = project(place, gathered, bands, keep, got, design)
    mine = run(sum_pieces, [(8, 2 * coefs + 128)], exchange(pieces, "tm", groups), close=(0,))
    other = lax.ppermute(mine, "tm", [(i, i ^ 2) for i in range(blocks_t)])
    grad, alpha, norms = run(
        step_piece, [(8, coefs), (8, 128), (32, 128)], place, mine, other, old, keep=(0,), close=(1, 2, 3), away=(2,)
    )
    norms = exchange(norms, "coef")
    new_solution, new_residual = run(
        update,
        [solution.shape, residual.shape],
        alpha,
        solution,
        direction,
        residual,
        predicted,
        close=(0, 4),
        away=(0, 1),
    )
    pieces = run(direction_piece, [(64, coefs)], place, norms, grad, old, direction, keep=(0, 4), close=(1, 2, 3))
    return new_solution.T, new_residual.T, exchange(pieces, "tm", groups).T


def solution(mesh):
    return jax.shard_map(
        per_device,
        mesh=mesh,
        in_specs=(
            P("tm", "coef"),
            P("tm", None),
            P("coef", None),
            P("coef", None),
            P("coef", None),
            P("tm", None),
        ),
        out_specs=(P("coef", None), P("tm", None), P("coef", None)),
        check_vma=False,
    )
```

```python
import jax
import jax.numpy as jnp
from jax import lax
from jax.experimental import pallas as pl
from jax.experimental.pallas import tpu as pltpu
from jax.sharding import PartitionSpec as P


BLOCK = 256
NN = (((1,), (0,)), ((), ()))
NT = (((1,), (1,)), ((), ()))
F32, BF16 = jnp.float32, jnp.bfloat16


def split(values):
    high = values.astype(BF16)
    return high, (values - high.astype(F32)).astype(BF16)


def times(left, right, dims):
    high, low = split(left)
    count = left.shape[0]
    first = lax.dot_general(jnp.concatenate([high, low], axis=0), right[0], dims, preferred_element_type=F32)
    return first[:count] + first[count:] + lax.dot_general(high, right[1], dims, preferred_element_type=F32)


def joined(first, second, axis):
    return tuple(jnp.concatenate([a, b], axis=axis) for a, b in zip(first, second, strict=True))


def skew(rows):
    return pltpu.roll(rows, 0, 1, stride=1, stride_axis=0)


def as_row(column):
    shape = (column.shape[0], 128)
    pick = lax.broadcasted_iota(jnp.int32, shape, 0) == lax.broadcasted_iota(jnp.int32, shape, 1)
    return jnp.sum(jnp.where(pick, jnp.broadcast_to(column, shape), 0.0), axis=0, keepdims=True)


def row_squares(values):
    total = values[:, :128] * values[:, :128]
    for k in range(128, values.shape[1], 128):
        total = total + values[:, k : k + 128] * values[:, k : k + 128]
    return as_row(jnp.sum(total, axis=1, keepdims=True))


def as_column(row, first, count):
    shape = (count, 128)
    pick = lax.broadcasted_iota(jnp.int32, shape, 1) == lax.broadcasted_iota(jnp.int32, shape, 0) + first
    return jnp.sum(jnp.where(pick, jnp.broadcast_to(row[:1], shape), 0.0), axis=1, keepdims=True)


def collect(rows):
    tile, old = rows[:8], rows[8:9]
    for m in range(1, 32):
        tile = tile + rows[9 * m : 9 * m + 8]
        old = old + rows[9 * m + 8 : 9 * m + 9]
    return tile, jnp.broadcast_to(old, (8, 128))


def chunk(tile, rim):
    return jnp.concatenate([tile, rim] * 32, axis=0)


def band(whitening, rim, residual, design):
    taps = jnp.concatenate([whitening, rim[:BLOCK]], axis=0)
    lag = lax.broadcasted_iota(jnp.int32, (BLOCK, BLOCK), 0)
    lane = lax.broadcasted_iota(jnp.int32, (BLOCK, BLOCK), 1)
    mirror = jnp.where((lag + lane) % BLOCK == 0, 1.0, 0.0).astype(BF16)
    high, low = split(taps)
    least = (taps - high.astype(F32) - low.astype(F32)).astype(BF16)
    count = taps.shape[0]
    turned = lax.dot_general(jnp.concatenate([high, low, least], axis=0), mirror, NN, preferred_element_type=F32)
    turned = turned[:count] + turned[count : 2 * count] + turned[2 * count :]
    same, before = [], []
    for b in range(3):
        full = skew(turned[BLOCK * b : BLOCK * (b + 1)])
        same.append(split(jnp.where(lane <= lag, full, 0.0)))
        before.append(split(jnp.where(lane > lag, full, 0.0)))
    res = [residual[:, :BLOCK], residual[:, BLOCK:], rim[BLOCK:]]
    back = [
        times(jnp.concatenate(res[b : b + 2], axis=1), joined(same[b], before[b + 1], 0), NN) for b in range(2)
    ]
    bands = [jnp.stack([m[k] for m in kind]) for kind in (same, before) for k in range(2)]
    return *bands, times(jnp.concatenate(back, axis=1), split(design()), NN)


def whiten_and_project(odd, gathered, same_high, same_low, before_high, before_low, keep, got, design):
    def block(halves, row, swap=0):
        return jnp.concatenate(
            [
                jnp.concatenate([gathered[16 * m + row : 16 * m + row + 8] for m in (8 * i + (j ^ swap) for i in halves)], axis=1)
                for j in range(8)
            ],
            axis=0,
        )

    same = [(same_high[b], same_low[b]) for b in range(3)]
    before = [(before_high[b], before_low[b]) for b in range(3)]
    plain = [
        jnp.where(odd, block((2, 3), 8), block((2, 3), 8, 2)),
        block((0, 1), 0),
        block((2, 3), 0),
        jnp.where(odd, block((0, 1), 8, 2), block((0, 1), 8)),
    ]
    pred = [
        times(jnp.concatenate(plain[b : b + 2], axis=1), joined(before[b], same[b], 1), NT) for b in range(3)
    ]
    own = jnp.concatenate(pred[:2], axis=1)
    energy = jnp.broadcast_to(row_squares(own), (64, 128))
    spread = [
        times(jnp.concatenate(pred[b : b + 2], axis=1), joined(same[b], before[b + 1], 0), NN) for b in range(2)
    ]
    left = jnp.concatenate(spread, axis=1)
    parts = []
    for k in range(2 * keep.shape[1] // BLOCK):
        parts.append(times(left, split(design(k)), NN))
    return jnp.concatenate([keep + got, *parts, energy], axis=1), own


def sum_pieces(pieces):
    half = (pieces.shape[1] - 128) // 3
    part = [pieces[8 * m : 8 * m + 8] for m in range(8)]
    back = [part[k][:, :half] + part[k + 2][:, :half] + part[k + 4][:, :half] + part[k + 6][:, :half] for k in range(2)]
    total = part[0][:, half:]
    for m in range(1, 8):
        total = total + part[m][:, half:]
    return jnp.concatenate([*back, total], axis=1)


def upper(place):
    return (place[0] & 1) == 1


def halves_of(values, swap):
    half = values.shape[1] // 2
    first, second = values[:, :half], values[:, half:]
    return jnp.where(swap, second, first), jnp.where(swap, first, second)


def own_group(place):
    return (lax.shift_right_logical(place[0], 2) * 2 + (place[0] & 1)) * 8


def step_piece(place, mine, other, old):
    total = mine + other
    count = (total.shape[1] - 128) // 2
    alpha = old / total[:, 2 * count :]
    alpha = jnp.where(lax.broadcasted_iota(jnp.int32, alpha.shape, 1) < 64, alpha, 0.0)
    grad = total[:, :count] - as_column(alpha, own_group(place), 8) * total[:, count : 2 * count]
    return grad, alpha, jnp.broadcast_to(row_squares(grad), (32, 128))


def direction_piece(place, norms, grad, old, direction):
    norm = jnp.sum(norms, axis=0, keepdims=True)
    beta = as_column(norm, 0, 8) / as_column(old, own_group(place), 8)
    mine = direction[pl.ds(pl.multiple_of(own_group(place), 8), 8), :]
    return jnp.concatenate([grad + beta * mine] * 8, axis=0)


def update(alpha, solution, direction, residual, predicted):
    step = as_column(alpha, 0, 64)
    return solution + step * direction, residual - step * predicted


def run(function, outs, *args, keep=(), close=(), away=()):
    def kernel(*refs):
        values = [r if k in keep else r[...] for k, r in enumerate(refs[: len(args)])]
        results = function(*values)
        results = results if isinstance(results, tuple) else (results,)
        for ref, value in zip(refs[len(args) :], results, strict=True):
            ref[...] = value

    spaces = [pltpu.SMEM if a.dtype == jnp.int32 else pltpu.VMEM for a in args]
    args = [near(a) if k in close else a for k, a in enumerate(args)]
    outs = [s if isinstance(s, tuple) and isinstance(s[0], tuple) else (s, F32) for s in outs]
    got = pl.pallas_call(
        kernel,
        out_shape=[(pltpu.HBM if k in away else pltpu.VMEM)(s, d) for k, (s, d) in enumerate(outs)],
        in_specs=[pl.BlockSpec(memory_space=s) for s in spaces],
        out_specs=[pl.BlockSpec(memory_space=pltpu.VMEM) for _ in outs],
        compiler_params=pltpu.CompilerParams(vmem_limit_bytes=24 << 20),
    )(*args)
    return got if len(outs) > 1 else got[0]


def near(array):
    return pltpu.with_memory_space_constraint(array, pltpu.VMEM)


def far(array):
    return pltpu.with_memory_space_constraint(array, pltpu.HBM)


LIMIT = pltpu.CompilerParams(vmem_limit_bytes=24 << 20)
HBM, VMEM = pl.BlockSpec(memory_space=pltpu.HBM), pl.BlockSpec(memory_space=pltpu.VMEM)


def predict(direction, design, gradient_prev, whitening, residual):
    def kernel(direction, design, gradient_prev, whitening, residual, rows, rim, dir_v, des_v, old_v, rows_v, sems):
        def copy(source, target, k):
            copies.append(pltpu.make_async_copy(source, target, sems.at[k]))
            copies[-1].start()

        copies = []
        copy(direction, dir_v, 0)
        copy(gradient_prev, old_v, 1)
        for i in range(4):
            copy(design.at[128 * i : 128 * i + 128], des_v.at[128 * i : 128 * i + 128], 2 + i)
        copies[0].wait()
        left = dir_v[...]
        copies[1].wait()
        old = row_squares(old_v[...])
        for m in range(32):
            rows_v[9 * m + 8 : 9 * m + 9] = old
        for i in range(4):
            copies[2 + i].wait()
            if i == 2:
                rims = [
                    pltpu.make_async_copy(whitening.at[:BLOCK], rim.at[:BLOCK], sems.at[6]),
                    pltpu.make_async_copy(residual.at[:, :BLOCK], rim.at[BLOCK:], sems.at[7]),
                ]
                for rows_out in rims:
                    rows_out.start()
            part = times(left, split(des_v[128 * i : 128 * i + 128]), NT)
            for j in range(8):
                first = 9 * (8 * i + j)
                rows_v[first : first + 8] = part[8 * j : 8 * j + 8]
            copy(rows_v.at[72 * i : 72 * i + 72], rows.at[72 * i : 72 * i + 72], 8 + i)
        for rows_out in rims + copies[6:]:
            rows_out.wait()

    return pl.pallas_call(
        kernel,
        out_shape=[
            pltpu.HBM((9 * 32, 128), F32),
            pltpu.VMEM((BLOCK + 64, BLOCK), F32),
        ],
        in_specs=[HBM] * 5,
        out_specs=[HBM, VMEM],
        scratch_shapes=[
            pltpu.VMEM(direction.shape, F32),
            pltpu.VMEM(design.shape, F32),
            pltpu.VMEM(gradient_prev.shape, F32),
            pltpu.VMEM((9 * 32, 128), F32),
            pltpu.SemaphoreType.DMA((12,)),
        ],
        compiler_params=LIMIT,
        name="predict",
    )(*[far(a) for a in (direction, design, gradient_prev, whitening, residual)])


def banded(place, whitening, rim, residual, design):
    def kernel(place, rim, whitening, residual, design, b0, b1, b2, b3, keep, send, tap_v, res_v, des_v, sems):
        copies = [
            pltpu.make_async_copy(source, target, sems.at[k])
            for k, (source, target) in enumerate(((whitening, tap_v), (residual, res_v), (design, des_v)))
        ]
        for copy in copies:
            copy.start()
        for copy in copies[:2]:
            copy.wait()

        def fetched():
            copies[2].wait()
            return des_v[...]

        b0[...], b1[...], b2[...], b3[...], back = band(tap_v[...], rim[...], res_v[...], fetched)
        keep[...], send[...] = halves_of(back, upper(place))

    args = (whitening, residual, design)
    return pl.pallas_call(
        kernel,
        out_shape=[pltpu.VMEM((3, BLOCK, BLOCK), BF16)] * 4 + [pltpu.VMEM((64, design.shape[1] // 2), F32)] * 2,
        in_specs=[pl.BlockSpec(memory_space=pltpu.SMEM), VMEM] + [HBM] * 3,
        out_specs=[VMEM] * 6,
        scratch_shapes=[pltpu.VMEM(a.shape, F32) for a in args] + [pltpu.SemaphoreType.DMA((3,))],
        compiler_params=LIMIT,
        name="band",
    )(place, near(rim), *[far(a) for a in args])


def project(place, gathered, bands, keep, got, design):
    count = design.shape[1] // BLOCK

    def kernel(place, gathered, b0, b1, b2, b3, keep, got, design, pieces, predicted, des_v, sems):
        copies = []
        for k in range(count):
            cut = pl.ds(BLOCK * k, BLOCK)
            copies.append(pltpu.make_async_copy(design.at[:, cut], des_v.at[:, cut], sems.at[k]))
            copies[-1].start()

        def fetched(k):
            copies[k].wait()
            return des_v[:, BLOCK * k : BLOCK * (k + 1)]

        pieces[...], predicted[...] = whiten_and_project(
            (place[0] & 1) == 1, gathered[...], b0[...], b1[...], b2[...], b3[...], keep[...], got[...], fetched
        )

    return pl.pallas_call(
        kernel,
        out_shape=[pltpu.VMEM((64, design.shape[1] // 2 * 3 + 128), F32), pltpu.VMEM((64, design.shape[0]), F32)],
        in_specs=[pl.BlockSpec(memory_space=pltpu.SMEM)] + [VMEM] * 7 + [HBM],
        out_specs=[VMEM] * 2,
        scratch_shapes=[pltpu.VMEM(design.shape, F32), pltpu.SemaphoreType.DMA((count,))],
        compiler_params=LIMIT,
        name="whiten_and_project",
    )(place, near(gathered), *[near(b) for b in bands], near(keep), near(got), far(design))


def exchange(rows, axis, groups=None):
    return lax.all_to_all(rows, axis, 0, 0, axis_index_groups=groups, tiled=True)


def neighbours(blocks_t, blocks_c, step):
    pairs = []
    for t in range(blocks_t):
        for c in range(blocks_c):
            to = t + step(c)
            if 0 <= to < blocks_t:
                pairs.append((t * blocks_c + c, to * blocks_c + (c if t // 2 == to // 2 else c ^ 2)))
    return pairs


def per_device(design, whitening, solution, direction, gradient_prev, residual):
    blocks_t, blocks_c = lax.axis_size("tm"), lax.axis_size("coef")
    coefs = design.shape[1]
    solution, direction, gradient_prev, residual = solution.T, direction.T, gradient_prev.T, residual.T
    groups = [[4 * x + 2 * z + k for x in range(4) for k in range(2)] for z in range(2)]
    t = lax.axis_index("tm").astype(jnp.int32)
    place = t[None]
    rows, rim = predict(direction, design, gradient_prev, whitening, residual)
    rows = exchange(rows.reshape(32, 9 * 128), "coef").reshape(9 * 32, 128)
    rim = lax.ppermute(rim, ("tm", "coef"), neighbours(blocks_t, blocks_c, lambda c: -1))
    *bands, keep, send = banded(place, whitening, rim, residual, design)
    tile, old = run(collect, [(8, 128), (8, 128)], rows, close=(0,))
    rim_tile = lax.ppermute(
        tile, ("tm", "coef"), neighbours(blocks_t, blocks_c, lambda c: 1 if c >= blocks_c // 2 else -1)
    )
    gathered = exchange(run(chunk, [(16 * 32, 128)], tile, rim_tile, close=(0, 1), away=(0,)), "coef")
    got = lax.ppermute(send, "tm", [(i, i ^ 1) for i in range(blocks_t)])
    pieces, predicted = project(place, gathered, bands, keep, got, design)
    mine = run(sum_pieces, [(8, 2 * coefs + 128)], exchange(pieces, "tm", groups), close=(0,))
    other = lax.ppermute(mine, "tm", [(i, i ^ 2) for i in range(blocks_t)])
    grad, alpha, norms = run(
        step_piece, [(8, coefs), (8, 128), (32, 128)], place, mine, other, old, keep=(0,), close=(1, 2, 3), away=(2,)
    )
    norms = exchange(norms, "coef")
    new_solution, new_residual = run(
        update,
        [solution.shape, residual.shape],
        alpha,
        solution,
        direction,
        residual,
        predicted,
        close=(0, 4),
        away=(0, 1),
    )
    pieces = run(direction_piece, [(64, coefs)], place, norms, grad, old, direction, keep=(0, 4), close=(1, 2, 3))
    return new_solution.T, new_residual.T, exchange(pieces, "tm", groups).T


def solution(mesh):
    return jax.shard_map(
        per_device,
        mesh=mesh,
        in_specs=(
            P("tm", "coef"),
            P("tm", None),
            P("coef", None),
            P("coef", None),
            P("coef", None),
            P("tm", None),
        ),
        out_specs=(P("coef", None), P("tm", None), P("coef", None)),
        check_vma=False,
    )
```
